512 devices in a mesh: row: 64 (over x, z), col: 8 (over y, core).
Axes of the slice: x: 4, y: 4, z: 16, core: 2. Of those that a mesh axis runs over, the one named last changes fastest.
Arguments:
- pending: bfloat16 [65536, 8, 1024], P('row', 'col'), may hold values from -5 to 5
- panel: bfloat16 [65536, 2, 1024], P('row', None, 'col'), may hold values from -0.1875 to 0.1875
- panel_scale: float32 [65536, 2], P('row'), may hold values from 0.1 to 1
- inverse_blocks: bfloat16 [2, 1024, 1024], P(None, 'col'), as said below
Outputs:
- remaining: bfloat16 [65536, 8, 1024], P('row', 'col')
- solved: bfloat16 [2, 1024, 1024], P(None, 'col')
The draws below stay inside these ranges and needn't reach their ends.
Inputs may be any that keep to these rules, and one draw needn't show every extreme that they name: `inverse_blocks`: each block is lower triangular with a positive diagonal, the inverse of a diagonal block of a Cholesky factor.
All inputs are finite; a program needn't handle non-finite values.
Results may differ from the reference program's by a relative error of at most 0.023.
Values may be sent and summed in bfloat16 or wider, within the bound.
A program may use at most 64 MiB of HBM per device.

```python
import math
import jax
import jax.numpy as jnp
from jax import lax

NB = 1024
NRHS = 1024
R = 1
ROWS = 65536
N_ROW = 64
N_COL = 8


def draw_inverse_blocks(key, part):
    key_low = jax.random.fold_in(key, 11)
    key_diag = jax.random.fold_in(key, 23)
    lower = jax.random.normal(key_low, (2, NB, NB), jnp.float32) * (1.5 / jnp.sqrt(jnp.float32(NB)))
    diag = jnp.exp(jax.random.uniform(key_diag, (2, NB), jnp.float32, jnp.log(0.5), jnp.log(2.0)))
    index = jnp.arange(NB)
    strict = index[:, None] > index[None, :]
    eye = (index[:, None] == index[None, :]).astype(jnp.float32)
    whole = jnp.where(strict[None], lower, 0.0) + diag[:, :, None] * eye[None]
    return whole.astype(jnp.bfloat16)


def steps_of(stream_key, shape, cuts, low, top_value):
    def one(position, blocks):
        draws = jax.random.uniform(jax.random.fold_in(jax.random.fold_in(stream_key, 6), position), (blocks,), jnp.float32, low / len(cuts), top_value / len(cuts))
        return jnp.repeat(jnp.exp(draws), shape[position] // blocks).reshape((-1,) + (1,) * (len(shape) - position - 1))

    factor_of = one(*cuts[0])
    for cut in cuts[1:]:
        factor_of = factor_of * one(*cut)
    return factor_of


def normal_values(stream_key, shape, scale, limit, cuts=(), kind=jnp.bfloat16):
    entries = scale * jax.random.normal(stream_key, shape, jnp.float32)
    if cuts:
        entries = entries * steps_of(stream_key, shape, cuts, -0.22, 0.18)
    return jnp.clip(entries, -limit, limit).astype(kind)


def setup_inputs(seed: int = 0) -> dict:
    arg_keys = jax.random.split(jax.random.key(seed), 5)
    pending = normal_values(arg_keys[0], (ROWS, N_COL, NRHS), 0.35, 5.0, ((0, 64), (1, 8)))
    panel = normal_values(arg_keys[1], (ROWS, 2, NB), NB ** -0.5, 0.1875, ((0, 64), (2, 8)))
    panel_scale = jnp.clip(jnp.exp(math.log(1.0) - 2.3025851 * jax.random.uniform(arg_keys[2], (ROWS, 2), jnp.float32) ** steps_of(arg_keys[2], (ROWS, 2), ((0, 64),), -0.2, 0.2)), 0.1, 1.0)
    inverse_blocks = draw_inverse_blocks(jax.random.fold_in(arg_keys[4], 71), 0)
    return dict(pending=pending, panel=panel, panel_scale=panel_scale, inverse_blocks=inverse_blocks)


def reference(pending, panel, panel_scale, inverse_blocks):
    cols_dev = NB // N_COL
    current = pending.reshape(N_ROW, R, NB, N_COL, NRHS)
    blocks = panel.reshape(N_ROW, R, NB, 2, N_COL, cols_dev)
    scales = panel_scale.reshape(N_ROW, R, NB, 2)
    slot_ids = jnp.arange(R, dtype=jnp.int32)
    solved_list = []
    for k in range(2):
        fan = jnp.sum(current[k, 0].astype(jnp.float32), axis=1)
        fan_rounded = fan.astype(jnp.bfloat16)
        solution = jnp.dot(inverse_blocks[k], fan_rounded, preferred_element_type=jnp.float32).astype(jnp.bfloat16)
        solved_list.append(solution)
        pieces = solution.reshape(N_COL, cols_dev, NRHS).astype(jnp.float32)

        def update_row(items):
            row_index, cur, blk, scl = items
            term = jnp.einsum("sicj,cjn->sicn", blk[:, :, k].astype(jnp.float32), pieces)
            newer = (cur.astype(jnp.float32) - scl[:, :, k][:, :, None, None] * term).astype(jnp.bfloat16)
            global_ids = slot_ids * N_ROW + row_index
            keep = (global_ids > k)[:, None, None, None]
            return jnp.where(keep, newer, cur)

        current = lax.map(update_row, (jnp.arange(N_ROW, dtype=jnp.int32), current, blocks, scales))
    remaining = current.reshape(N_ROW * R * NB, N_COL, NRHS)
    return remaining, jnp.stack(solved_list)
```

```python
import functools

import jax
import jax.numpy as jnp
from jax import lax
from jax.experimental import pallas as pl
from jax.experimental.pallas import tpu as pltpu
from jax.sharding import PartitionSpec as P

MESH = pl.DeviceIdType.MESH
NX, NY, NZ = 4, 4, 16
BF = jnp.bfloat16
F32 = jnp.float32
FAR_FIRST = (8, 9, 7, 10, 6, 11, 5, 12, 4, 13, 3, 14, 2, 15, 1)


def comm_kernel(
    pend, scaled, linv, out,
    cur, xin, part, fan, linv_o, oblk, pmat,
    ld, xs, xr, ps, pr, as_, ar, ls, lr, zs, zr_, fs, fr,
):
    row, col = lax.axis_index("row"), lax.axis_index("col")
    x, z = row // NZ, row % NZ
    y, h = col // 2, col % 2
    other = 2 * y + (1 - h)
    even = x % 2 == 0

    def zrel(k):
        return (z - k + NZ) % NZ

    def lead_z(k):
        zr = zrel(k)
        second = jnp.where(even, 1, NZ - 1)
        return jnp.logical_or(zr == 0, zr == second)

    mine = h == x // 2
    second = jnp.where(even, 1, NZ - 1)

    def dev(xx, zz, cc):
        return (xx * NZ + zz, cc)

    source = [jnp.logical_and(x == 0, z == k) for k in range(2)]
    is_source = jnp.logical_or(source[0], source[1])

    @pl.when(is_source)
    def _():
        pltpu.make_async_copy(pend, cur, ld.at[0]).start()

    @pl.when(source[1])
    def _():
        pltpu.make_async_copy(scaled.at[:, pl.ds(0, 128)], pmat, ld.at[1]).start()

    bar = pltpu.get_barrier_semaphore()

    def hello(target):
        pl.semaphore_signal(bar, inc=1, device_id=target, device_id_type=MESH)

    hello((row, other))
    for d in range(1, NX):
        hello(dev((x + d) % NX, z, col))
    lead_col = 2 * y + x // 2
    expect = jnp.int32(1 + NX - 1)
    for k in range(2):
        for j in range(2):
            lz = (k + (0 if j == 0 else second)) % NZ
            @pl.when(z != lz)
            def _():
                hello(dev(x, lz, lead_col))
        lead = jnp.logical_and(lead_z(k), mine)
        for yd in range(1, NY):
            @pl.when(lead)
            def _():
                hello((row, 2 * ((y + yd) % NY) + h))
        for yd in range(NY):
            sy = (y + yd) % NY
            @pl.when(jnp.logical_and(lead, jnp.logical_or(jnp.logical_not(source[k]), sy != y)))
            def _():
                hello((k, 2 * sy + h))
        expect += jnp.where(lead, 2 * (NZ - 1) + NY - 1, 0)
        expect += jnp.where(source[k], jnp.where(h == 0, 4 * NY - 1, 4 * NY), 0)
    pl.semaphore_wait(bar, expect)

    def linv_copy(k):
        return pltpu.make_async_remote_copy(
            linv.at[k], linv_o.at[k], ls.at[k], lr.at[k], device_id=(row, other), device_id_type=MESH)

    gives = [jnp.logical_and(lead_z(k), jnp.logical_not(mine)) for k in range(2)]

    def half(i):
        return pl.ds(pl.multiple_of((4 * (1 - h) + i) * 128, 128), 128)

    def own(i):
        return pl.ds(pl.multiple_of((4 * h + i) * 128, 128), 128)

    def swap_copy(i):
        return pltpu.make_async_remote_copy(
            cur.at[:, half(i)], xin.at[i], xs.at[i], xr.at[i], device_id=(row, other), device_id_type=MESH)

    def scatter_copy(k, i, yd):
        zoff = 0 if i % 2 == 0 else (1 if i // 2 == 0 else NZ - 1)
        ty = (y + yd) % NY
        rows = pl.ds(pl.multiple_of(ty * 256, 256), 256)
        return pltpu.make_async_remote_copy(
            xin.at[i, rows], part.at[k, yd], ps.at[i, yd], pr.at[k, yd],
            device_id=dev(2 * h + i // 2, (k + zoff) % NZ, 2 * ty + h), device_id_type=MESH)

    def add_and_scatter(k):
        for i in range(4):
            swap_copy(i).wait_recv()

            def add(r, c):
                rows = pl.ds(pl.multiple_of(r * 256, 256), 256)
                xin[i, rows] = (cur[rows, own(i)].astype(F32) + xin[i, rows].astype(F32)).astype(BF)
                return c
            lax.fori_loop(0, 4, add, 0)
            for yd in range(NY):
                if i == 0 and yd == 0:
                    @pl.when(h == 0)
                    def _():
                        part[k, 0] = xin[0, pl.ds(pl.multiple_of(y * 256, 256), 256)]

                    @pl.when(h != 0)
                    def _():
                        scatter_copy(k, i, yd).start()
                else:
                    scatter_copy(k, i, yd).start()

    def gather_copy(k, yd):
        rows = pl.ds(pl.multiple_of(y * 256, 256), 256)
        return pltpu.make_async_remote_copy(
            fan.at[k, rows], fan.at[k, rows], as_.at[k, yd - 1], ar.at[k, yd - 1],
            device_id=(row, 2 * ((y + yd) % NY) + h), device_id_type=MESH)

    def piece(k, xx, j):
        return out.at[k, :, pl.ds(pl.multiple_of((2 * xx + j) * 128, 128), 128)]

    def my_j(k):
        return jnp.where(zrel(k) == 0, 0, 1)

    def line_copy(k, j, d, same):
        target = dev(x, (z + d) % NZ, col if same else other)
        src = piece(k, x, j) if same else oblk.at[k]
        return pltpu.make_async_remote_copy(
            src, piece(k, x, j), zs.at[k, d, 0 if same else 1], zr_.at[k, j],
            device_id=target, device_id_type=MESH)

    def lead_step(k):
        for yd in range(NY):
            if yd == 0:
                @pl.when(jnp.logical_not(source[k]))
                def _():
                    scatter_copy(k, 0, yd).wait_recv()
            else:
                scatter_copy(k, 0, yd).wait_recv()
        total = part[k, 0].astype(F32)
        for yd in range(1, NY):
            total += part[k, yd].astype(F32)
        fan[k, pl.ds(pl.multiple_of(y * 256, 256), 256)] = total.astype(BF)
        for yd in range(1, NY):
            gather_copy(k, yd).start()
        linv_copy(k).wait_recv()
        for yd in range(1, NY):
            gather_copy(k, yd).wait_recv()
        f = fan[k]
        oblk[k] = jnp.dot(linv_o[k], f, preferred_element_type=F32).astype(BF)
        block = jnp.dot(linv[k], f, preferred_element_type=F32).astype(BF)
        for j in range(2):
            @pl.when(my_j(k) == j)
            def _():
                out[k, :, pl.ds(pl.multiple_of((2 * x + j) * 128, 128), 128)] = block
                for d in FAR_FIRST:
                    line_copy(k, j, d, False).start()
                    line_copy(k, j, d, True).start()
                line_copy(k, j, 0, False).start()

    def spread_copy(k, j, d):
        tx = (x + d) % NX
        return pltpu.make_async_remote_copy(
            piece(k, x, j), piece(k, x, j), fs.at[k, j, d - 1], fr.at[k, j, d - 1],
            device_id=dev(tx, z, col), device_id_type=MESH)

    def spread_wait(k, j, d):
        fx = (x + NX - d) % NX
        return pltpu.make_async_remote_copy(
            piece(k, fx, j), piece(k, fx, j), fs.at[k, j, d - 1], fr.at[k, j, d - 1],
            device_id=dev(fx, z, col), device_id_type=MESH)

    for k in range(2):
        @pl.when(gives[k])
        def _():
            linv_copy(k).start()

    for k in range(2):
        @pl.when(source[k])
        def _():
            if k == 0:
                pltpu.make_async_copy(pend, cur, ld.at[0]).wait()
                for i in range(4):
                    swap_copy(i).start()
            else:
                for j in range(2):
                    for d in range(1, NX):
                        spread_wait(0, j, d).wait_recv()
                pltpu.make_async_copy(pend, cur, ld.at[0]).wait()
                pltpu.make_async_copy(scaled.at[:, pl.ds(0, 128)], pmat, ld.at[1]).wait()

                def update(cols):
                    def tile(r, c):
                        rows = pl.ds(pl.multiple_of(r * 256, 256), 256)
                        term = jnp.dot(pmat[rows], out[0, :, cols], preferred_element_type=F32)
                        cur[rows, cols] = (cur[rows, cols].astype(F32) - term).astype(BF)
                        return c
                    lax.fori_loop(0, 4, tile, 0)
                for i in range(4):
                    update(half(i))
                    swap_copy(i).start()
                for i in range(4):
                    update(own(i))
            add_and_scatter(k)

        lead = jnp.logical_and(lead_z(k), mine)

        @pl.when(lead)
        def _():
            lead_step(k)

        for j in range(2):
            @pl.when(jnp.logical_not(jnp.logical_and(lead, my_j(k) == j)))
            def _():
                line_copy(k, j, 0, False).wait_recv()
            for d in (2, 1, 3):
                spread_copy(k, j, d).start()

    for k in range(2):
        for j in range(2):
            for d in range(1, NX):
                if k == 0:
                    @pl.when(jnp.logical_not(source[1]))
                    def _():
                        spread_wait(k, j, d).wait_recv()
                else:
                    spread_wait(k, j, d).wait_recv()
                spread_copy(k, j, d).wait_send()

    for k in range(2):
        @pl.when(gives[k])
        def _():
            linv_copy(k).wait_send()

        @pl.when(source[k])
        def _():
            for i in range(4):
                swap_copy(i).wait_send()
                for yd in range(NY):
                    if i == 0 and yd == 0:
                        @pl.when(h != 0)
                        def _():
                            scatter_copy(k, i, yd).wait_send()
                    else:
                        scatter_copy(k, i, yd).wait_send()

        @pl.when(jnp.logical_and(lead_z(k), mine))
        def _():
            for yd in range(1, NY):
                gather_copy(k, yd).wait_send()
            for d in FAR_FIRST:
                line_copy(k, 0, d, False).wait_send()
                line_copy(k, 0, d, True).wait_send()
            line_copy(k, 0, 0, False).wait_send()


def update_kernel(pend, scaled, solved, out):
    for c in range(4):
        cols = slice(c * 256, (c + 1) * 256)
        term = jnp.dot(scaled[...], solved[:, cols], preferred_element_type=F32)
        out[:, cols] = (pend[:, cols].astype(F32) - term).astype(BF)


def body(pending, panel, panel_scale, inverse_blocks):
    row = lax.axis_index("row")
    rows, _, cols = pending.shape
    current = pending.reshape(rows, cols)
    active = (row > jnp.arange(2)).astype(F32)
    scaled = (panel.astype(F32) * (panel_scale * active)[:, :, None]).astype(BF).reshape(rows, 256)
    anyspec = pl.BlockSpec(memory_space=pl.ANY)
    vmem = pl.BlockSpec(memory_space=pltpu.VMEM)
    dma = pltpu.SemaphoreType.DMA
    solved = pl.pallas_call(
        comm_kernel,
        out_shape=jax.ShapeDtypeStruct((2, 128, cols), BF),
        in_specs=[anyspec, anyspec, vmem],
        out_specs=vmem,
        scratch_shapes=[
            pltpu.VMEM((rows, cols), BF),
            pltpu.VMEM((4, rows, 128), BF),
            pltpu.VMEM((2, NY, 256, 128), BF),
            pltpu.VMEM((2, rows, 128), BF),
            pltpu.VMEM((2, 128, cols), BF),
            pltpu.VMEM((2, 128, 128), BF),
            pltpu.VMEM((rows, 128), BF),
            dma((2,)), dma((4,)), dma((4,)), dma((4, NY)), dma((2, NY)),
            dma((2, NY - 1)), dma((2, NY - 1)), dma((2,)), dma((2,)),
            dma((2, NZ, 2)), dma((2, 2)), dma((2, 2, NX - 1)), dma((2, 2, NX - 1)),
        ],
        compiler_params=pltpu.CompilerParams(
            collective_id=0, has_side_effects=True, vmem_limit_bytes=32 << 20),
        name="substitute",
    )(current, scaled, inverse_blocks)
    tile = 256
    remaining = pl.pallas_call(
        update_kernel,
        grid=(rows // tile,),
        out_shape=jax.ShapeDtypeStruct((rows, cols), BF),
        in_specs=[
            pl.BlockSpec((tile, cols), lambda i: (i, 0)),
            pl.BlockSpec((tile, 256), lambda i: (i, 0)),
            pl.BlockSpec((256, cols), lambda i: (0, 0)),
        ],
        out_specs=pl.BlockSpec((tile, cols), lambda i: (i, 0)),
        compiler_params=pltpu.CompilerParams(vmem_limit_bytes=32 << 20),
        name="update",
    )(current, scaled, solved.reshape(256, cols))
    return remaining[:, None, :], solved


def solution(mesh):
    placed = (P("row", "col", None), P("row", None, "col"), P("row", None), P(None, "col", None))
    return jax.shard_map(
        body,
        mesh=mesh,
        in_specs=placed,
        out_specs=(P("row", "col", None), P(None, "col", None)),
        check_vma=False,
    )
```

```python
import functools

import jax
import jax.numpy as jnp
from jax import lax
from jax.experimental import pallas as pl
from jax.experimental.pallas import tpu as pltpu
from jax.sharding import PartitionSpec as P

MESH = pl.DeviceIdType.MESH
NX, NY, NZ = 4, 4, 16
BF = jnp.bfloat16
F32 = jnp.float32
FAR_FIRST = (8, 9, 7, 10, 6, 11, 5, 12, 4, 13, 3, 14, 2, 15, 1)


RELAYS = {0: (2, 6), 5: (4,), 2: (3,), 6: (7,)}
FIRST = (0, 1, 5)


def place(e):
    x = e // 2
    return x, (0 if e % 2 == 0 else (1 if x % 2 == 0 else NZ - 1)), x // 2


def comm_kernel(
    pend, panel, scale, linv, out, scaled,
    xin, part, fan, sol, prow, diff, linv_o, oblk,
    xs, xr, ps, pr, as_, ar, ls, lr, qs, qr, rs, zs, zr_, fs, fr,
):
    row, col = lax.axis_index("row"), lax.axis_index("col")
    x, z = row // NZ, row % NZ
    y, h = col // 2, col % 2
    other = 2 * y + (1 - h)
    second = jnp.where(x % 2 == 0, 1, NZ - 1)
    mine = h == x // 2
    lead_chip = jnp.logical_or(z == 0, z == second)
    lead = jnp.logical_and(lead_chip, mine)
    my_j = jnp.where(z == 0, 0, 1)
    my_e = jnp.where(lead, 2 * x + my_j, -1)
    source = [row == k for k in range(2)]
    my_rows = pl.ds(pl.multiple_of(y * 256, 256), 256)

    def dev(xx, zz, cc):
        return (xx * NZ + zz, cc)

    def solver(e, yy):
        ex, ez, eh = place(e)
        return dev(ex, ez, 2 * yy + eh)

    bar = pltpu.get_barrier_semaphore()

    def hello(target):
        pl.semaphore_signal(bar, inc=1, device_id=target, device_id_type=MESH)

    def both(p, q):
        return jnp.logical_and(p, q)

    def no(p):
        return jnp.logical_not(p)

    for yd in range(NY):
        sy = (y + yd) % NY
        if yd:
            @pl.when(lead)
            def _():
                hello((row, 2 * sy + h))
        for k in range(2):
            @pl.when(both(lead, no(source[k])) if yd == 0 else lead)
            def _():
                hello((k, 2 * sy + h))
        for e in FIRST:
            for hh in range(2):
                @pl.when(both(my_e == e, no(both(source[1], hh == h))) if yd == 0 else my_e == e)
                def _():
                    hello((1, 2 * sy + hh))
    for parent, children in RELAYS.items():
        for child in children:
            @pl.when(my_e == child)
            def _():
                hello(solver(parent, y))
    hello((row, other))
    lead_col = 2 * y + x // 2
    for lz in (0, second):
        @pl.when(z != lz)
        def _():
            hello(dev(x, lz, lead_col))
    for d in range(1, NX):
        hello(dev((x + d) % NX, z, col))
    expect = jnp.int32(1 + NX - 1) + jnp.where(lead, 2 * (NZ - 1) + NY - 1, 0)
    for k in range(2):
        expect += jnp.where(source[k], jnp.where(h == 0, 4 * NY - 1, 4 * NY), 0)
    expect += jnp.where(source[1], jnp.where(h == 0, 3 * NY - 1, 3 * NY), 0)
    for parent, children in RELAYS.items():
        expect += jnp.where(my_e == parent, len(children), 0)

    for k in range(2):
        active = jnp.where(row > k, 1.0, 0.0)

        def scale_rows(r, c):
            rows = pl.ds(pl.multiple_of(r * 256, 256), 256)
            s = jnp.broadcast_to(scale[k : k + 1, rows] * active, (128, 256)).T
            scaled[rows, k * 128 : (k + 1) * 128] = (panel[rows, k, :].astype(F32) * s).astype(BF)
            return c
        lax.fori_loop(0, 4, scale_rows, 0)

    pl.semaphore_wait(bar, expect)

    def remote(src, dst, send, recv, target):
        return pltpu.make_async_remote_copy(
            src, dst, send, recv, device_id=target, device_id_type=MESH)

    def linv_copy(k):
        return remote(linv.at[k], linv_o.at[k], ls.at[k], lr.at[k], (row, other))

    def lanes(i):
        return pl.ds(pl.multiple_of(i * 128, 128), 128)

    def swap_copy(i):
        return remote(pend.at[:, lanes(4 * (1 - h) + i)], xin.at[i], xs.at[i], xr.at[i], (row, other))

    def scatter_copy(k, i, yd):
        zz = 0 if i % 2 == 0 else (1 if i // 2 == 0 else NZ - 1)
        ty = (y + yd) % NY
        rows = pl.ds(pl.multiple_of(ty * 256, 256), 256)
        return remote(xin.at[i, rows], part.at[k, yd], ps.at[i, yd], pr.at[k, yd],
                      dev(2 * h + i // 2, zz, 2 * ty + h))

    def panel_copy(t, yd):
        ty = (y + yd) % NY
        rows = pl.ds(pl.multiple_of(ty * 256, 256), 256)
        return remote(scaled.at[rows, pl.ds(0, 128)], prow.at[:, lanes(col)], qs.at[t, yd], qr.at[col],
                      solver(FIRST[t], ty))

    def panel_wait(c):
        return remote(prow.at[:, lanes(c)], prow.at[:, lanes(c)], qs.at[0, 0], qr.at[c], (row, other))

    def relay_copy(child, n, c):
        return remote(prow.at[:, lanes(c)], prow.at[:, lanes(c)], rs.at[n, c], qr.at[c], solver(child, y))

    def gather_copy(buf, n, yd):
        return remote(buf.at[my_rows], buf.at[my_rows], as_.at[n, yd - 1], ar.at[n, yd - 1],
                      (row, 2 * ((y + yd) % NY) + h))

    def piece(k, xx, j):
        return out.at[k, :, lanes(2 * xx + j)]

    def line_copy(k, j, d, same):
        return remote(piece(k, x, j) if same else oblk.at[k], piece(k, x, j),
                      zs.at[k, d, 0 if same else 1], zr_.at[k, j],
                      dev(x, (z + d) % NZ, col if same else other))

    def spread_copy(k, j, d):
        return remote(piece(k, x, j), piece(k, x, j), fs.at[k, j, d - 1], fr.at[k, j, d - 1],
                      dev((x + d) % NX, z, col))

    def spread_wait(k, j, d):
        fx = (x + NX - d) % NX
        return remote(piece(k, fx, j), piece(k, fx, j), fs.at[k, j, d - 1], fr.at[k, j, d - 1],
                      dev(fx, z, col))

    def spread(k):
        for j in range(2):
            @pl.when(no(both(lead, my_j == j)))
            def _():
                line_copy(k, j, 0, False).wait_recv()
            for d in (2, 1, 3):
                spread_copy(k, j, d).start()

    def local_slot(k, i, yd):
        return i == k and yd == 0

    @pl.when(both(lead_chip, no(mine)))
    def _():
        for k in range(2):
            linv_copy(k).start()

    is_source = jnp.logical_or(source[0], source[1])

    @pl.when(is_source)
    def _():
        for i in range(4):
            swap_copy(i).start()

    @pl.when(source[1])
    def _():
        for t in range(3):
            for yd in range(NY):
                if t == 1 and yd == 0:
                    @pl.when(h == 0)
                    def _():
                        prow[:, lanes(col)] = scaled[my_rows, 0:128]

                    @pl.when(h != 0)
                    def _():
                        panel_copy(t, yd).start()
                else:
                    panel_copy(t, yd).start()

    @pl.when(is_source)
    def _():
        for i in range(4):
            swap_copy(i).wait_recv()

            def add(r, c):
                rows = pl.ds(pl.multiple_of(r * 256, 256), 256)
                xin[i, rows] = (pend[rows, lanes(4 * h + i)].astype(F32) + xin[i, rows].astype(F32)).astype(BF)
                return c
            lax.fori_loop(0, 4, add, 0)
            for k in range(2):
                @pl.when(source[k])
                def _():
                    for yd in range(NY):
                        if local_slot(k, i, yd):
                            @pl.when(h == 0)
                            def _():
                                part[k, 0] = xin[i, my_rows]

                            @pl.when(h != 0)
                            def _():
                                scatter_copy(k, i, yd).start()
                        else:
                            scatter_copy(k, i, yd).start()

    def reduced(k):
        @pl.when(no(source[k]))
        def _():
            scatter_copy(k, 0, 0).wait_recv()
        for yd in range(1, NY):
            scatter_copy(k, 0, yd).wait_recv()
        total = part[k, 0].astype(F32)
        for yd in range(1, NY):
            total += part[k, yd].astype(F32)
        return total

    def gather_start(buf, n):
        for yd in range(1, NY):
            gather_copy(buf, n, yd).start()

    def gather_wait(buf, n):
        for yd in range(1, NY):
            gather_copy(buf, n, yd).wait_recv()

    def solve(k):
        f = fan[k]
        block = jnp.dot(linv[k], f, preferred_element_type=F32).astype(BF)
        oblk[k] = jnp.dot(linv_o[k], f, preferred_element_type=F32).astype(BF)
        out[k, :, lanes(2 * x + my_j)] = block
        return block

    def line_start(k):
        for j in range(2):
            @pl.when(my_j == j)
            def _():
                for d in FAR_FIRST:
                    line_copy(k, j, d, False).start()
                    line_copy(k, j, d, True).start()
                line_copy(k, j, 0, False).start()

    @pl.when(lead)
    def _():
        fan[0, my_rows] = reduced(0).astype(BF)
        gather_start(fan.at[0], 0)
        for parent, children in RELAYS.items():
            @pl.when(my_e == parent)
            def _():
                for c in range(8):
                    panel_wait(c).wait_recv()
                    for n, child in enumerate(children):
                        relay_copy(child, n, c).start()
        for k in range(2):
            linv_copy(k).wait_recv()
        gather_wait(fan.at[0], 0)
        block = solve(0)
        sol[pl.ds(pl.multiple_of(col * 128, 128), 128)] = block
        sol[pl.ds(pl.multiple_of(other * 128, 128), 128)] = oblk[0]
        gather_start(sol, 1)
        line_start(0)
        diff[...] = reduced(1)
        relaying = jnp.bool_(False)
        for parent in RELAYS:
            relaying = jnp.logical_or(relaying, my_e == parent)
        for c in range(8):
            @pl.when(no(jnp.logical_or(relaying, both(source[1], c == col))))
            def _():
                panel_wait(c).wait_recv()
        gather_wait(sol, 1)
        fan[1, my_rows] = (
            diff[...] - jnp.dot(prow[...], sol[...], preferred_element_type=F32)).astype(BF)
        gather_start(fan.at[1], 2)
        spread(0)
        gather_wait(fan.at[1], 2)
        solve(1)
        line_start(1)

    @pl.when(no(lead))
    def _():
        spread(0)
    spread(1)

    for k in range(2):
        for j in range(2):
            for d in range(1, NX):
                spread_wait(k, j, d).wait_recv()

    for k in range(2):
        for j in range(2):
            for d in range(1, NX):
                spread_copy(k, j, d).wait_send()

    @pl.when(both(lead_chip, no(mine)))
    def _():
        for k in range(2):
            linv_copy(k).wait_send()

    for k in range(2):
        @pl.when(source[k])
        def _():
            for i in range(4):
                swap_copy(i).wait_send()
                for yd in range(NY):
                    if local_slot(k, i, yd):
                        @pl.when(h != 0)
                        def _():
                            scatter_copy(k, i, yd).wait_send()
                    else:
                        scatter_copy(k, i, yd).wait_send()

    @pl.when(source[1])
    def _():
        for t in range(3):
            for yd in range(NY):
                if t == 1 and yd == 0:
                    @pl.when(h != 0)
                    def _():
                        panel_copy(t, yd).wait_send()
                else:
                    panel_copy(t, yd).wait_send()

    @pl.when(lead)
    def _():
        for n, buf in enumerate((fan.at[0], sol, fan.at[1])):
            for yd in range(1, NY):
                gather_copy(buf, n, yd).wait_send()
        for k in range(2):
            for d in FAR_FIRST:
                line_copy(k, 0, d, False).wait_send()
                line_copy(k, 0, d, True).wait_send()
            line_copy(k, 0, 0, False).wait_send()
    for parent, children in RELAYS.items():
        @pl.when(my_e == parent)
        def _():
            for c in range(8):
                for n, child in enumerate(children):
                    relay_copy(child, n, c).wait_send()


def update_kernel(pend, scaled, solved, out):
    for c in range(4):
        cols = slice(c * 256, (c + 1) * 256)
        term = jnp.dot(scaled[...], solved[:, cols], preferred_element_type=F32)
        out[:, cols] = (pend[:, cols].astype(F32) - term).astype(BF)


def body(pending, panel, panel_scale, inverse_blocks):
    rows, _, cols = pending.shape
    current = pending.reshape(rows, cols)
    vmem = pl.BlockSpec(memory_space=pltpu.VMEM)
    dma = pltpu.SemaphoreType.DMA
    solved, scaled = pl.pallas_call(
        comm_kernel,
        out_shape=(jax.ShapeDtypeStruct((2, 128, cols), BF), jax.ShapeDtypeStruct((rows, 256), BF)),
        in_specs=[vmem] * 4,
        out_specs=(vmem, vmem),
        scratch_shapes=[
            pltpu.VMEM((4, rows, 128), BF),
            pltpu.VMEM((2, NY, 256, 128), BF),
            pltpu.VMEM((2, rows, 128), BF),
            pltpu.VMEM((rows, 128), BF),
            pltpu.VMEM((256, rows), BF),
            pltpu.VMEM((256, 128), F32),
            pltpu.VMEM((2, 128, cols), BF),
            pltpu.VMEM((2, 128, 128), BF),
            dma((4,)), dma((4,)), dma((4, NY)), dma((2, NY)),
            dma((3, NY - 1)), dma((3, NY - 1)), dma((2,)), dma((2,)),
            dma((3, NY)), dma((8,)), dma((2, 8)),
            dma((2, NZ, 2)), dma((2, 2)), dma((2, 2, NX - 1)), dma((2, 2, NX - 1)),
        ],
        compiler_params=pltpu.CompilerParams(
            collective_id=0, has_side_effects=True, vmem_limit_bytes=32 << 20),
        name="substitute",
    )(current, panel, panel_scale.T, inverse_blocks)
    tile = 256
    remaining = pl.pallas_call(
        update_kernel,
        grid=(rows // tile,),
        out_shape=jax.ShapeDtypeStruct((rows, cols), BF),
        in_specs=[
            pl.BlockSpec((tile, cols), lambda i: (i, 0)),
            pl.BlockSpec((tile, 256), lambda i: (i, 0)),
            pl.BlockSpec((256, cols), lambda i: (0, 0)),
        ],
        out_specs=pl.BlockSpec((tile, cols), lambda i: (i, 0)),
        compiler_params=pltpu.CompilerParams(vmem_limit_bytes=32 << 20),
        name="update",
    )(current, scaled, solved.reshape(256, cols))
    return remaining[:, None, :], solved


def solution(mesh):
    placed = (P("row", "col", None), P("row", None, "col"), P("row", None), P(None, "col", None))
    return jax.shard_map(
        body,
        mesh=mesh,
        in_specs=placed,
        out_specs=(P("row", "col", None), P(None, "col", None)),
        check_vma=False,
    )
```

```python
import functools

import jax
import jax.numpy as jnp
from jax import lax
from jax.experimental import pallas as pl
from jax.experimental.pallas import tpu as pltpu
from jax.sharding import PartitionSpec as P

MESH = pl.DeviceIdType.MESH
NX, NY, NZ = 4, 4, 16
BF = jnp.bfloat16
F32 = jnp.float32
DIRECT = (6, 10, 8, 4, 12, 3, 13, 2, 14, 1, 15)
RELAYED = (5, 7, 9, 11)


RELAYS = {0: (2, 6), 5: (4,), 2: (3,), 6: (7,)}
FIRST = (0, 1, 5)


def place(e):
    x = e // 2
    return x, (0 if e % 2 == 0 else (1 if x % 2 == 0 else NZ - 1)), x // 2


def comm_kernel(
    pend, panel_in, scale_in, linv_in, out, scaled,
    panel, scale, linv, pown, xin, part, fan, sol, prow, diff, linv_o, oblk,
    ready, ld, lp, xs, xr, ps, pr, as_, ar, ls, lr, qs, qr, rs, zs, zr_, ts, fs, fr,
):
    row, col = lax.axis_index("row"), lax.axis_index("col")
    x, z = row // NZ, row % NZ
    y, h = col // 2, col % 2
    other = 2 * y + (1 - h)
    second = jnp.where(x % 2 == 0, 1, NZ - 1)
    mine = h == x // 2
    lead_chip = jnp.logical_or(z == 0, z == second)
    lead = jnp.logical_and(lead_chip, mine)
    my_j = jnp.where(z == 0, 0, 1)
    my_e = jnp.where(lead, 2 * x + my_j, -1)
    source = [row == k for k in range(2)]
    my_rows = pl.ds(pl.multiple_of(y * 256, 256), 256)

    def dev(xx, zz, cc):
        return (xx * NZ + zz, cc)

    def solver(e, yy):
        ex, ez, eh = place(e)
        return dev(ex, ez, 2 * yy + eh)

    is_source = jnp.logical_or(source[0], source[1])

    def lanes(i):
        return pl.ds(pl.multiple_of(i * 128, 128), 128)

    def load(n):
        src, dst = ((panel_in, panel), (scale_in, scale), (linv_in, linv))[n]
        return pltpu.make_async_copy(src, dst, ld.at[n])

    def load_own(i):
        return pltpu.make_async_copy(pend.at[:, lanes(4 * h + i)], pown.at[i], lp.at[i])

    load(0).start()
    load(1).start()

    @pl.when(lead)
    def _():
        load(2).start()

    @pl.when(is_source)
    def _():
        for i in range(4):
            load_own(i).start()

    bar = pltpu.get_barrier_semaphore()

    def hello(target):
        pl.semaphore_signal(bar, inc=1, device_id=target, device_id_type=MESH)

    def both(p, q):
        return jnp.logical_and(p, q)

    def no(p):
        return jnp.logical_not(p)

    for yd in range(NY):
        sy = (y + yd) % NY
        if yd:
            @pl.when(lead)
            def _():
                hello((row, 2 * sy + h))
        for k in range(2):
            @pl.when(both(lead, no(source[k])) if yd == 0 else lead)
            def _():
                hello((k, 2 * sy + h))
        for e in FIRST:
            for hh in range(2):
                @pl.when(both(my_e == e, no(both(source[1], hh == h))) if yd == 0 else my_e == e)
                def _():
                    hello((1, 2 * sy + hh))
    for parent, children in RELAYS.items():
        for child in children:
            @pl.when(my_e == child)
            def _():
                hello(solver(parent, y))
    hello((row, other))
    lead_col = 2 * y + x // 2
    line_z = (jnp.int32(0), second)
    away = [(z - lz + NZ) % NZ for lz in line_z]

    def among(v, values):
        hit = v == values[0]
        for w in values[1:]:
            hit = jnp.logical_or(hit, v == w)
        return hit

    direct = [among(a, DIRECT) for a in away]
    relayed = [among(a, RELAYED) for a in away]
    relays = [among(a, (6, 10)) for a in away]
    my_leads = jnp.where(direct[0], 1, 0) + jnp.where(direct[1], 1, 0)
    for j in range(2):
        @pl.when(relayed[j])
        def _():
            step = jnp.where(jnp.logical_or(away[j] == 7, away[j] == 11), NZ - 1, 1)
            hello(dev(x, (z + step) % NZ, col))
        my_leads += jnp.where(relays[j], 2, 0)

    @pl.when(lead)
    def _():
        for d in DIRECT:
            for hh in range(2):
                hello(dev(x, (z + d) % NZ, 2 * y + hh))
    for d in range(1, NX):
        hello(dev((x + d) % NX, z, col))
    expect = 1 + NX - 1 + my_leads + jnp.where(lead, NY - 1, 0)
    for k in range(2):
        expect += jnp.where(source[k], jnp.where(h == 0, 4 * NY - 1, 4 * NY), 0)
    expect += jnp.where(source[1], jnp.where(h == 0, 3 * NY - 1, 3 * NY), 0)
    for parent, children in RELAYS.items():
        expect += jnp.where(my_e == parent, len(children), 0)

    def scale_panel():
        load(0).wait()
        load(1).wait()
        for k in range(2):
            active = jnp.where(row > k, 1.0, 0.0)

            def scale_rows(r, c):
                rows = pl.ds(pl.multiple_of(r * 256, 256), 256)
                s = jnp.broadcast_to(scale[k : k + 1, rows] * active, (128, 256)).T
                scaled[rows, k * 128 : (k + 1) * 128] = (panel[rows, k, :].astype(F32) * s).astype(BF)
                return c
            lax.fori_loop(0, 4, scale_rows, 0)

    early = jnp.logical_or(source[1], no(jnp.logical_or(source[0], lead)))

    @pl.when(early)
    def _():
        scale_panel()

    pl.semaphore_wait(bar, expect)

    for j in range(2):
        @pl.when(direct[j])
        def _():
            pl.semaphore_signal(
                ready, inc=1, device_id=dev(x, line_z[j], lead_col), device_id_type=MESH)

    def remote(src, dst, send, recv, target):
        return pltpu.make_async_remote_copy(
            src, dst, send, recv, device_id=target, device_id_type=MESH)

    def linv_copy(k):
        return remote(linv_in.at[k], linv_o.at[k], ls.at[k], lr.at[k], (row, other))

    def swap_copy(i):
        return remote(pend.at[:, lanes(4 * (1 - h) + i)], xin.at[i], xs.at[i], xr.at[i], (row, other))

    def scatter_copy(k, i, yd):
        zz = 0 if i % 2 == 0 else (1 if i // 2 == 0 else NZ - 1)
        ty = (y + yd) % NY
        rows = pl.ds(pl.multiple_of(ty * 256, 256), 256)
        return remote(xin.at[i, rows], part.at[k, yd], ps.at[i, yd], pr.at[k, yd],
                      dev(2 * h + i // 2, zz, 2 * ty + h))

    def panel_copy(t, yd):
        ty = (y + yd) % NY
        rows = pl.ds(pl.multiple_of(ty * 256, 256), 256)
        return remote(scaled.at[rows, pl.ds(0, 128)], prow.at[:, lanes(col)], qs.at[t, yd], qr.at[col],
                      solver(FIRST[t], ty))

    def panel_wait(c):
        return remote(prow.at[:, lanes(c)], prow.at[:, lanes(c)], qs.at[0, 0], qr.at[c], (row, other))

    def relay_copy(child, n, c):
        return remote(prow.at[:, lanes(c)], prow.at[:, lanes(c)], rs.at[n, c], qr.at[c], solver(child, y))

    def gather_copy(buf, n, yd):
        return remote(buf.at[my_rows], buf.at[my_rows], as_.at[n, yd - 1], ar.at[n, yd - 1],
                      (row, 2 * ((y + yd) % NY) + h))

    def piece(k, xx, j):
        return out.at[k, :, lanes(2 * xx + j)]

    def line_copy(k, j, d, same):
        return remote(piece(k, x, j) if same else oblk.at[k], piece(k, x, j),
                      zs.at[k, d, 0 if same else 1], zr_.at[k, j],
                      dev(x, (z + d) % NZ, col if same else other))

    def pass_copy(k, j, n):
        return remote(piece(k, x, j), piece(k, x, j), ts.at[k, n], zr_.at[k, j],
                      dev(x, (z + (1, NZ - 1)[n]) % NZ, col))

    def spread_copy(k, j, d):
        return remote(piece(k, x, j), piece(k, x, j), fs.at[k, j, d - 1], fr.at[k, j, d - 1],
                      dev((x + d) % NX, z, col))

    def spread_wait(k, j, d):
        fx = (x + NX - d) % NX
        return remote(piece(k, fx, j), piece(k, fx, j), fs.at[k, j, d - 1], fr.at[k, j, d - 1],
                      dev(fx, z, col))

    def spread(k):
        for j in range(2):
            @pl.when(no(both(lead, my_j == j)))
            def _():
                line_copy(k, j, 0, False).wait_recv()

            @pl.when(relays[j])
            def _():
                for n in range(2):
                    pass_copy(k, j, n).start()
            for d in (2, 1, 3):
                spread_copy(k, j, d).start()

    def local_slot(k, i, yd):
        return i == k and yd == 0

    @pl.when(both(lead_chip, no(mine)))
    def _():
        for k in range(2):
            linv_copy(k).start()

    @pl.when(is_source)
    def _():
        for i in range(4):
            swap_copy(i).start()

    @pl.when(source[1])
    def _():
        for t in range(3):
            for yd in range(NY):
                if t == 1 and yd == 0:
                    @pl.when(h == 0)
                    def _():
                        prow[:, lanes(col)] = scaled[my_rows, 0:128]

                    @pl.when(h != 0)
                    def _():
                        panel_copy(t, yd).start()
                else:
                    panel_copy(t, yd).start()

    @pl.when(is_source)
    def _():
        for i in range(4):
            load_own(i).wait()
            swap_copy(i).wait_recv()

            def add(r, c):
                rows = pl.ds(pl.multiple_of(r * 256, 256), 256)
                xin[i, rows] = (pown[i, rows].astype(F32) + xin[i, rows].astype(F32)).astype(BF)
                return c
            lax.fori_loop(0, 4, add, 0)
            for k in range(2):
                @pl.when(source[k])
                def _():
                    for yd in range(NY):
                        if local_slot(k, i, yd):
                            @pl.when(h == 0)
                            def _():
                                part[k, 0] = xin[i, my_rows]

                            @pl.when(h != 0)
                            def _():
                                scatter_copy(k, i, yd).start()
                        else:
                            scatter_copy(k, i, yd).start()

    def reduced(k):
        @pl.when(no(source[k]))
        def _():
            scatter_copy(k, 0, 0).wait_recv()
        for yd in range(1, NY):
            scatter_copy(k, 0, yd).wait_recv()
        total = part[k, 0].astype(F32)
        for yd in range(1, NY):
            total += part[k, yd].astype(F32)
        return total

    def gather_start(buf, n):
        for yd in (2, 1, 3):
            gather_copy(buf, n, yd).start()

    def gather_wait(buf, n):
        for yd in range(1, NY):
            gather_copy(buf, n, yd).wait_recv()

    def solve(k):
        f = fan[k]
        block = jnp.dot(linv[k], f, preferred_element_type=F32).astype(BF)
        oblk[k] = jnp.dot(linv_o[k], f, preferred_element_type=F32).astype(BF)
        out[k, :, lanes(2 * x + my_j)] = block
        return block

    def line_start(k):
        for j in range(2):
            @pl.when(my_j == j)
            def _():
                for d in DIRECT:
                    line_copy(k, j, d, False).start()
                    line_copy(k, j, d, True).start()
                line_copy(k, j, 0, False).start()

    @pl.when(lead)
    def _():
        fan[0, my_rows] = reduced(0).astype(BF)
        gather_start(fan.at[0], 0)
        for parent, children in RELAYS.items():
            @pl.when(my_e == parent)
            def _():
                for c in range(8):
                    panel_wait(c).wait_recv()
                    for n, child in enumerate(children):
                        relay_copy(child, n, c).start()
        for k in range(2):
            linv_copy(k).wait_recv()
        load(2).wait()
        gather_wait(fan.at[0], 0)
        block = solve(0)
        sol[pl.ds(pl.multiple_of(col * 128, 128), 128)] = block
        sol[pl.ds(pl.multiple_of(other * 128, 128), 128)] = oblk[0]
        gather_start(sol, 1)
        pl.semaphore_wait(ready, 2 * len(DIRECT))
        line_start(0)
        diff[...] = reduced(1)
        relaying = jnp.bool_(False)
        for parent in RELAYS:
            relaying = jnp.logical_or(relaying, my_e == parent)
        for c in range(8):
            @pl.when(no(jnp.logical_or(relaying, both(source[1], c == col))))
            def _():
                panel_wait(c).wait_recv()
        gather_wait(sol, 1)
        fan[1, my_rows] = (
            diff[...] - jnp.dot(prow[...], sol[...], preferred_element_type=F32)).astype(BF)
        gather_start(fan.at[1], 2)
        spread(0)
        gather_wait(fan.at[1], 2)
        solve(1)
        line_start(1)

    @pl.when(no(lead))
    def _():
        spread(0)

    @pl.when(no(early))
    def _():
        scale_panel()
    spread(1)

    for k in range(2):
        for j in range(2):
            for d in range(1, NX):
                spread_wait(k, j, d).wait_recv()

    for k in range(2):
        for j in range(2):
            for d in range(1, NX):
                spread_copy(k, j, d).wait_send()

            @pl.when(relays[j])
            def _():
                for n in range(2):
                    pass_copy(k, j, n).wait_send()

    @pl.when(both(lead_chip, no(mine)))
    def _():
        for k in range(2):
            linv_copy(k).wait_send()

    for k in range(2):
        @pl.when(source[k])
        def _():
            for i in range(4):
                swap_copy(i).wait_send()
                for yd in range(NY):
                    if local_slot(k, i, yd):
                        @pl.when(h != 0)
                        def _():
                            scatter_copy(k, i, yd).wait_send()
                    else:
                        scatter_copy(k, i, yd).wait_send()

    @pl.when(source[1])
    def _():
        for t in range(3):
            for yd in range(NY):
                if t == 1 and yd == 0:
                    @pl.when(h != 0)
                    def _():
                        panel_copy(t, yd).wait_send()
                else:
                    panel_copy(t, yd).wait_send()

    @pl.when(lead)
    def _():
        for n, buf in enumerate((fan.at[0], sol, fan.at[1])):
            for yd in range(1, NY):
                gather_copy(buf, n, yd).wait_send()
        for k in range(2):
            for d in DIRECT:
                line_copy(k, 0, d, False).wait_send()
                line_copy(k, 0, d, True).wait_send()
            line_copy(k, 0, 0, False).wait_send()
    for parent, children in RELAYS.items():
        @pl.when(my_e == parent)
        def _():
            for c in range(8):
                for n, child in enumerate(children):
                    relay_copy(child, n, c).wait_send()


def update_kernel(pend, scaled, solved, out, solved_out, done, sem):
    tiles = done.shape[0]
    size = done.shape[1]
    last = pltpu.make_async_copy(solved, solved_out, sem.at[tiles])
    last.start()

    def store(i):
        return pltpu.make_async_copy(
            done.at[i], out.at[pl.ds(pl.multiple_of(i * size, size), size)], sem.at[i])

    def tile(i, c):
        rows = pl.ds(pl.multiple_of(i * size, size), size)
        for n in range(4):
            cols = slice(n * 256, (n + 1) * 256)
            term = jnp.dot(scaled[rows], solved[:, cols], preferred_element_type=F32)
            done[i, :, cols] = (pend[rows, cols].astype(F32) - term).astype(BF)
        store(i).start()
        return c
    lax.fori_loop(0, tiles, tile, 0)
    for i in range(tiles):
        store(i).wait()
    last.wait()


def body(pending, panel, panel_scale, inverse_blocks):
    rows, _, cols = pending.shape
    current = pending.reshape(rows, cols)
    vmem = pl.BlockSpec(memory_space=pltpu.VMEM)
    hbm = pl.BlockSpec(memory_space=pltpu.HBM)
    dma = pltpu.SemaphoreType.DMA
    solved, scaled = pl.pallas_call(
        comm_kernel,
        out_shape=(jax.ShapeDtypeStruct((2, 128, cols), BF), jax.ShapeDtypeStruct((rows, 256), BF)),
        in_specs=[hbm] * 4,
        out_specs=(vmem, vmem),
        scratch_shapes=[
            pltpu.VMEM((rows, 2, 128), BF),
            pltpu.VMEM((2, rows), F32),
            pltpu.VMEM((2, 128, rows), BF),
            pltpu.VMEM((4, rows, 128), BF),
            pltpu.VMEM((4, rows, 128), BF),
            pltpu.VMEM((2, NY, 256, 128), BF),
            pltpu.VMEM((2, rows, 128), BF),
            pltpu.VMEM((rows, 128), BF),
            pltpu.VMEM((256, rows), BF),
            pltpu.VMEM((256, 128), F32),
            pltpu.VMEM((2, 128, cols), BF),
            pltpu.VMEM((2, 128, 128), BF),
            pltpu.SemaphoreType.REGULAR, dma((3,)), dma((4,)),
            dma((4,)), dma((4,)), dma((4, NY)), dma((2, NY)),
            dma((3, NY - 1)), dma((3, NY - 1)), dma((2,)), dma((2,)),
            dma((3, NY)), dma((8,)), dma((2, 8)),
            dma((2, NZ, 2)), dma((2, 2)), dma((2, 2)), dma((2, 2, NX - 1)), dma((2, 2, NX - 1)),
        ],
        compiler_params=pltpu.CompilerParams(
            collective_id=0, has_side_effects=True, vmem_limit_bytes=32 << 20),
        name="substitute",
    )(*(pltpu.with_memory_space_constraint(v, pltpu.HBM)
        for v in (current, panel, panel_scale.T, inverse_blocks)))
    remaining, solved = pl.pallas_call(
        update_kernel,
        out_shape=(jax.ShapeDtypeStruct((rows, cols), BF), jax.ShapeDtypeStruct((256, cols), BF)),
        in_specs=[vmem] * 3,
        out_specs=(hbm, hbm),
        scratch_shapes=[pltpu.VMEM((8, rows // 8, cols), BF), dma((9,))],
        compiler_params=pltpu.CompilerParams(vmem_limit_bytes=32 << 20),
        name="update",
    )(current, scaled, solved.reshape(256, cols))
    return remaining[:, None, :], solved.reshape(2, 128, cols)


def solution(mesh):
    placed = (P("row", "col", None), P("row", None, "col"), P("row", None), P(None, "col", None))
    return jax.shard_map(
        body,
        mesh=mesh,
        in_specs=placed,
        out_specs=(P("row", "col", None), P(None, "col", None)),
        check_vma=False,
    )
```

```python
import functools

import jax
import jax.numpy as jnp
from jax import lax
from jax.experimental import pallas as pl
from jax.experimental.pallas import tpu as pltpu
from jax.sharding import PartitionSpec as P

MESH = pl.DeviceIdType.MESH
NX, NY, NZ = 4, 4, 16
BF = jnp.bfloat16
F32 = jnp.float32
DIRECT = (6, 10, 8, 4, 12, 3, 13, 2, 14, 1, 15)
RELAYED = (5, 7, 9, 11)


CHILDREN = {8: (6, 5, 1), 6: (7, 0, 4), 5: (2,), 1: (3,)}
ADDERS = ((1, 1), (0, 2), (0, 3), (3, 1))


ORDER = ((1, 2, 3, 0), (1, 2, 3, 0))


def place(e):
    x = e // 2
    return x, (0 if e % 2 == 0 else (1 if x % 2 == 0 else NZ - 1)), x // 2


def node_place(n):
    if n == 8:
        return 3, 1, 0
    x, z, core = place(n)
    return x, z, 1 - core


def comm_kernel(
    pend, panel_in, scale_in, linv_in, out, scaled,
    panel, scale, linv, pown, xin, part, fan, sol, prow, acc, diff, oblk,
    ready, ld, lp, xs, xr, ps, pr, as_, ar, ls, lr, qs, qr, rs, us, ds_, dr, zs, zr_, ts, fs, fr,
):
    row, col = lax.axis_index("row"), lax.axis_index("col")
    x, z = row // NZ, row % NZ
    y, h = col // 2, col % 2
    other = 2 * y + (1 - h)
    second = jnp.where(x % 2 == 0, 1, NZ - 1)
    mine = h == x // 2
    lead_chip = jnp.logical_or(z == 0, z == second)
    lead = jnp.logical_and(lead_chip, mine)
    my_j = jnp.where(z == 0, 0, 1)
    my_e = jnp.where(lead, 2 * x + my_j, -1)
    source = [row == k for k in range(2)]
    my_node = jnp.where(jnp.logical_and(lead_chip, jnp.logical_not(mine)), 2 * x + my_j, -1)
    my_node = jnp.where(jnp.logical_and(row == 3 * NZ + 1, h == 0), 8, my_node)
    my_add = jnp.int32(-1)
    for i, (ax, az) in enumerate(ADDERS):
        my_add = jnp.where(row == ax * NZ + az, i, my_add)
    adder = my_add >= 0
    my_rows = pl.ds(pl.multiple_of(y * 256, 256), 256)

    def dev(xx, zz, cc):
        return (xx * NZ + zz, cc)

    def solver(e, yy):
        ex, ez, eh = place(e)
        return dev(ex, ez, 2 * yy + eh)

    is_source = jnp.logical_or(source[0], source[1])

    def node(n, yy):
        nx, nz, nh = node_place(n)
        return dev(nx, nz, 2 * yy + nh)

    def lanes(i):
        return pl.ds(pl.multiple_of(i * 128, 128), 128)

    def load(n):
        src, dst = ((panel_in, panel), (scale_in, scale), (linv_in, linv.at[:, pl.ds(0, 128)]))[n]
        return pltpu.make_async_copy(src, dst, ld.at[n])

    def load_own(i):
        return pltpu.make_async_copy(pend.at[:, lanes(4 * h + i)], pown.at[i], lp.at[i])

    load(0).start()
    load(1).start()

    @pl.when(lead)
    def _():
        load(2).start()

    @pl.when(is_source)
    def _():
        for i in range(4):
            load_own(i).start()

    bar = pltpu.get_barrier_semaphore()

    def hello(target):
        pl.semaphore_signal(bar, inc=1, device_id=target, device_id_type=MESH)

    def both(p, q):
        return jnp.logical_and(p, q)

    def no(p):
        return jnp.logical_not(p)

    for yd in range(NY):
        sy = (y + yd) % NY
        if yd:
            @pl.when(lead)
            def _():
                hello((row, 2 * sy + h))
        @pl.when(both(lead, no(source[0])) if yd == 0 else lead)
        def _():
            hello((0, 2 * sy + h))

        @pl.when(adder)
        def _():
            hello((1, 2 * sy + h))

        @pl.when(my_node == 8)
        def _():
            for hh in range(2):
                hello((1, 2 * sy + hh))
    for parent, children in CHILDREN.items():
        for child in children:
            @pl.when(my_node == child)
            def _():
                hello(node(parent, y))
    for i, (ax, az) in enumerate(ADDERS):
        @pl.when(both(lead, my_e % 4 == i))
        def _():
            hello(dev(ax, az, col))
    hello((row, other))
    lead_col = 2 * y + x // 2
    line_z = (jnp.int32(0), second)
    away = [(z - lz + NZ) % NZ for lz in line_z]

    def among(v, values):
        hit = v == values[0]
        for w in values[1:]:
            hit = jnp.logical_or(hit, v == w)
        return hit

    direct = [among(a, DIRECT) for a in away]
    relayed = [among(a, RELAYED) for a in away]
    relays = [among(a, (6, 10)) for a in away]
    my_leads = jnp.where(direct[0], 1, 0) + jnp.where(direct[1], 1, 0)
    for j in range(2):
        @pl.when(relayed[j])
        def _():
            step = jnp.where(jnp.logical_or(away[j] == 7, away[j] == 11), NZ - 1, 1)
            hello(dev(x, (z + step) % NZ, col))
        my_leads += jnp.where(relays[j], 2, 0)

    @pl.when(lead)
    def _():
        for d in DIRECT:
            for hh in range(2):
                hello(dev(x, (z + d) % NZ, 2 * y + hh))
    for d in range(1, NX):
        hello(dev((x + d) % NX, z, col))
    expect = 1 + NX - 1 + my_leads + jnp.where(lead, NY - 1, 0)
    expect += jnp.where(source[0], jnp.where(h == 0, 4 * NY - 1, 4 * NY), 0)
    expect += jnp.where(source[1], 4 * NY + NY, 0)
    expect += jnp.where(adder, 1, 0)
    for parent, children in CHILDREN.items():
        expect += jnp.where(my_node == parent, len(children), 0)

    def scale_panel():
        load(0).wait()
        load(1).wait()
        for k in range(2):
            active = jnp.where(row > k, 1.0, 0.0)

            def scale_rows(r, c):
                rows = pl.ds(pl.multiple_of(r * 256, 256), 256)
                s = jnp.broadcast_to(scale[k : k + 1, rows] * active, (128, 256)).T
                scaled[rows, k * 128 : (k + 1) * 128] = (panel[rows, k, :].astype(F32) * s).astype(BF)
                return c
            lax.fori_loop(0, 4, scale_rows, 0)

    early = jnp.logical_or(source[1], no(jnp.logical_or(source[0], lead)))

    @pl.when(early)
    def _():
        scale_panel()

    pl.semaphore_wait(bar, expect)

    for j in range(2):
        @pl.when(direct[j])
        def _():
            pl.semaphore_signal(
                ready, inc=1, device_id=dev(x, line_z[j], lead_col), device_id_type=MESH)

    def remote(src, dst, send, recv, target):
        return pltpu.make_async_remote_copy(
            src, dst, send, recv, device_id=target, device_id_type=MESH)

    def linv_copy(k):
        return remote(linv_in.at[k], linv.at[k, pl.ds(128, 128)], ls.at[k], lr.at[k], (row, other))

    def swap_copy(i):
        return remote(pend.at[:, lanes(4 * (1 - h) + i)], xin.at[i], xs.at[i], xr.at[i], (row, other))

    def scatter_copy(k, i, yd):
        zz = 0 if i % 2 == 0 else (1 if i // 2 == 0 else NZ - 1)
        tx = 2 * h + i // 2
        if k == 1:
            tx, zz = ADDERS[i]
        ty = (y + yd) % NY
        rows = pl.ds(pl.multiple_of(ty * 256, 256), 256)
        return remote(xin.at[i, rows], part.at[k, yd], ps.at[i, yd], pr.at[k, yd],
                      dev(tx, zz, 2 * ty + h))

    def panel_copy(yd):
        ty = (y + yd) % NY
        rows = pl.ds(pl.multiple_of(ty * 256, 256), 256)
        return remote(scaled.at[rows, pl.ds(0, 128)], prow.at[:, lanes(col)], qs.at[yd], qr.at[col],
                      node(8, ty))

    def panel_wait(c):
        return remote(prow.at[:, lanes(c)], prow.at[:, lanes(c)], qs.at[0], qr.at[c], (row, other))

    def relay_copy(child, n, c):
        return remote(prow.at[:, lanes(c)], prow.at[:, lanes(c)], rs.at[n, c], qr.at[c], node(child, y))

    def mate_copy(c):
        return remote(prow.at[:, lanes(c)], prow.at[:, lanes(c)], us.at[c], qr.at[c], (row, other))

    def diff_copy(i):
        tz = 0 if i % 2 == 0 else (1 if i // 2 == 0 else NZ - 1)
        return remote(acc, diff, ds_, dr, dev(2 * h + i // 2, tz, col))

    def gather_copy(buf, n, yd):
        return remote(buf.at[my_rows], buf.at[my_rows], as_.at[n, yd - 1], ar.at[n, yd - 1],
                      (row, 2 * ((y + yd) % NY) + h))

    def piece(k, xx, j):
        return out.at[k, :, lanes(2 * xx + j)]

    def line_copy(k, j, d, same):
        return remote(piece(k, x, j) if same else oblk.at[k], piece(k, x, j),
                      zs.at[k, d, 0 if same else 1], zr_.at[k, j],
                      dev(x, (z + d) % NZ, col if same else other))

    def pass_copy(k, j, n):
        return remote(piece(k, x, j), piece(k, x, j), ts.at[k, n], zr_.at[k, j],
                      dev(x, (z + (1, NZ - 1)[n]) % NZ, col))

    def spread_copy(k, j, d):
        return remote(piece(k, x, j), piece(k, x, j), fs.at[k, j, d - 1], fr.at[k, j, d - 1],
                      dev((x + d) % NX, z, col))

    def spread_wait(k, j, d):
        fx = (x + NX - d) % NX
        return remote(piece(k, fx, j), piece(k, fx, j), fs.at[k, j, d - 1], fr.at[k, j, d - 1],
                      dev(fx, z, col))

    def spread(k):
        for j in range(2):
            @pl.when(no(both(lead, my_j == j)))
            def _():
                line_copy(k, j, 0, False).wait_recv()

            @pl.when(relays[j])
            def _():
                for n in range(2):
                    pass_copy(k, j, n).start()
            for d in (2, 1, 3):
                spread_copy(k, j, d).start()

    def unless_local(k, i, yd, action, local=None):
        if not (k == 0 and i == 0 and yd == 0):
            action()
        else:
            pl.when(h != 0)(action)
            if local:
                pl.when(h == 0)(local)

    @pl.when(both(lead_chip, no(mine)))
    def _():
        for k in range(2):
            linv_copy(k).start()

    @pl.when(is_source)
    def _():
        for k in range(2):
            @pl.when(source[k])
            def _():
                for i in ORDER[k]:
                    swap_copy(i).start()

    @pl.when(source[1])
    def _():
        for yd in range(NY):
            panel_copy(yd).start()

    for k in range(2):
        @pl.when(source[k])
        def _():
            for i in ORDER[k]:
                load_own(i).wait()
                swap_copy(i).wait_recv()

                def add(r, c):
                    rows = pl.ds(pl.multiple_of(r * 256, 256), 256)
                    xin[i, rows] = (pown[i, rows].astype(F32) + xin[i, rows].astype(F32)).astype(BF)
                    return c
                lax.fori_loop(0, 4, add, 0)

                def keep():
                    part[k, 0] = xin[i, my_rows]
                for yd in (2, 1, 3, 0):
                    unless_local(k, i, yd, lambda: scatter_copy(k, i, yd).start(), keep)

    def reduced(k):
        if k == 1:
            scatter_copy(k, 0, 0).wait_recv()
        else:
            @pl.when(no(source[0]))
            def _():
                scatter_copy(k, 0, 0).wait_recv()
        for yd in range(1, NY):
            scatter_copy(k, 0, yd).wait_recv()
        total = part[k, 0].astype(F32)
        for yd in range(1, NY):
            total += part[k, yd].astype(F32)
        return total

    def gather_start(buf, n):
        for yd in (2, 1, 3):
            gather_copy(buf, n, yd).start()

    def gather_wait(buf, n):
        for yd in range(1, NY):
            gather_copy(buf, n, yd).wait_recv()

    def solve(k):
        blocks = jnp.dot(linv[k], fan[k], preferred_element_type=F32).astype(BF)
        oblk[k] = blocks[128:]
        out[k, :, lanes(2 * x + my_j)] = blocks[:128]
        return blocks

    def line_start(k):
        for j in range(2):
            @pl.when(my_j == j)
            def _():
                for d in DIRECT:
                    line_copy(k, j, d, False).start()
                    line_copy(k, j, d, True).start()
                line_copy(k, j, 0, False).start()

    def add_up():
        @pl.when(adder)
        def _():
            acc[...] = reduced(1)
            for i in range(4):
                @pl.when(my_add == i)
                def _():
                    diff_copy(i).start()

    @pl.when(my_node >= 0)
    def _():
        for c in range(8):
            panel_wait(c).wait_recv()
            for parent, children in CHILDREN.items():
                @pl.when(my_node == parent)
                def _():
                    for n, child in enumerate(children):
                        relay_copy(child, n, c).start()

            @pl.when(my_node != 8)
            def _():
                mate_copy(c).start()

    @pl.when(lead)
    def _():
        fan[0, my_rows] = reduced(0).astype(BF)
        gather_start(fan.at[0], 0)
        for k in range(2):
            linv_copy(k).wait_recv()
        load(2).wait()
        gather_wait(fan.at[0], 0)
        blocks = solve(0)
        sol[pl.ds(pl.multiple_of(col * 128, 128), 128)] = blocks[:128]
        sol[pl.ds(pl.multiple_of(other * 128, 128), 128)] = blocks[128:]
        gather_start(sol, 1)
        pl.semaphore_wait(ready, 2 * len(DIRECT))
        line_start(0)
        diff_copy(0).wait_recv()
        for c in range(8):
            panel_wait(c).wait_recv()
        gather_wait(sol, 1)
        fan[1, my_rows] = (
            diff[...] - jnp.dot(prow[...], sol[...], preferred_element_type=F32)).astype(BF)
        gather_start(fan.at[1], 2)
        spread(0)
        gather_wait(fan.at[1], 2)
        solve(1)
        line_start(1)

    @pl.when(no(lead))
    def _():
        add_up()
        spread(0)

    @pl.when(no(early))
    def _():
        scale_panel()
    spread(1)

    for k in range(2):
        for j in range(2):
            for d in range(1, NX):
                spread_wait(k, j, d).wait_recv()

    for k in range(2):
        for j in range(2):
            for d in range(1, NX):
                spread_copy(k, j, d).wait_send()

            @pl.when(relays[j])
            def _():
                for n in range(2):
                    pass_copy(k, j, n).wait_send()

    @pl.when(both(lead_chip, no(mine)))
    def _():
        for k in range(2):
            linv_copy(k).wait_send()

    for k in range(2):
        @pl.when(source[k])
        def _():
            for i in range(4):
                swap_copy(i).wait_send()
                for yd in range(NY):
                    unless_local(k, i, yd, lambda: scatter_copy(k, i, yd).wait_send())

    @pl.when(source[1])
    def _():
        for yd in range(NY):
            panel_copy(yd).wait_send()

    @pl.when(lead)
    def _():
        for n, buf in enumerate((fan.at[0], sol, fan.at[1])):
            for yd in range(1, NY):
                gather_copy(buf, n, yd).wait_send()
        for k in range(2):
            for d in DIRECT:
                line_copy(k, 0, d, False).wait_send()
                line_copy(k, 0, d, True).wait_send()
            line_copy(k, 0, 0, False).wait_send()
    @pl.when(adder)
    def _():
        diff_copy(0).wait_send()

    @pl.when(my_node >= 0)
    def _():
        for c in range(8):
            for parent, children in CHILDREN.items():
                @pl.when(my_node == parent)
                def _():
                    for n, child in enumerate(children):
                        relay_copy(child, n, c).wait_send()

            @pl.when(my_node != 8)
            def _():
                mate_copy(c).wait_send()


def update_kernel(pend, scaled, solved, out, solved_out, done, sem):
    tiles = done.shape[0]
    size = done.shape[2]
    last = pltpu.make_async_copy(solved, solved_out, sem.at[tiles])
    last.start()

    def store(i):
        return pltpu.make_async_copy(
            done.at[i], out.at[:, pl.ds(pl.multiple_of(i * size, size), size)], sem.at[i])

    def tile(i, c):
        cols = pl.ds(pl.multiple_of(i * size, size), size)
        term = jnp.dot(scaled[...], solved[:, cols], preferred_element_type=F32)
        done[i] = (pend[:, cols].astype(F32) - term).astype(BF)
        store(i).start()
        return c
    lax.fori_loop(0, tiles, tile, 0)
    for i in range(tiles):
        store(i).wait()
    last.wait()


def body(pending, panel, panel_scale, inverse_blocks):
    rows, _, cols = pending.shape
    current = pending.reshape(rows, cols)
    vmem = pl.BlockSpec(memory_space=pltpu.VMEM)
    hbm = pl.BlockSpec(memory_space=pltpu.HBM)
    dma = pltpu.SemaphoreType.DMA
    solved, scaled = pl.pallas_call(
        comm_kernel,
        out_shape=(jax.ShapeDtypeStruct((2, 128, cols), BF), jax.ShapeDtypeStruct((rows, 256), BF)),
        in_specs=[hbm] * 4,
        out_specs=(vmem, vmem),
        scratch_shapes=[
            pltpu.VMEM((rows, 2, 128), BF),
            pltpu.VMEM((2, rows), F32),
            pltpu.VMEM((2, 256, rows), BF),
            pltpu.VMEM((4, rows, 128), BF),
            pltpu.VMEM((4, rows, 128), BF),
            pltpu.VMEM((2, NY, 256, 128), BF),
            pltpu.VMEM((2, rows, 128), BF),
            pltpu.VMEM((rows, 128), BF),
            pltpu.VMEM((256, rows), BF),
            pltpu.VMEM((256, 128), F32),
            pltpu.VMEM((256, 128), F32),
            pltpu.VMEM((2, 128, 128), BF),
            pltpu.SemaphoreType.REGULAR, dma((3,)), dma((4,)),
            dma((4,)), dma((4,)), dma((4, NY)), dma((2, NY)),
            dma((3, NY - 1)), dma((3, NY - 1)), dma((2,)), dma((2,)),
            dma((NY,)), dma((8,)), dma((3, 8)), dma((8,)), dma, dma,
            dma((2, NZ, 2)), dma((2, 2)), dma((2, 2)), dma((2, 2, NX - 1)), dma((2, 2, NX - 1)),
        ],
        compiler_params=pltpu.CompilerParams(
            collective_id=0, has_side_effects=True, vmem_limit_bytes=32 << 20),
        name="substitute",
    )(*(pltpu.with_memory_space_constraint(v, pltpu.HBM)
        for v in (current, panel, panel_scale.T, inverse_blocks)))
    remaining, solved = pl.pallas_call(
        update_kernel,
        out_shape=(jax.ShapeDtypeStruct((rows, cols), BF), jax.ShapeDtypeStruct((256, cols), BF)),
        in_specs=[vmem] * 3,
        out_specs=(hbm, hbm),
        scratch_shapes=[pltpu.VMEM((4, rows, cols // 4), BF), dma((5,))],
        compiler_params=pltpu.CompilerParams(vmem_limit_bytes=32 << 20),
        name="update",
    )(current, scaled, solved.reshape(256, cols))
    return remaining[:, None, :], solved.reshape(2, 128, cols)


def solution(mesh):
    placed = (P("row", "col", None), P("row", None, "col"), P("row", None), P(None, "col", None))
    return jax.shard_map(
        body,
        mesh=mesh,
        in_specs=placed,
        out_specs=(P("row", "col", None), P(None, "col", None)),
        check_vma=False,
    )
```

```python
import functools

import jax
import jax.numpy as jnp
from jax import lax
from jax.experimental import pallas as pl
from jax.experimental.pallas import tpu as pltpu
from jax.sharding import PartitionSpec as P

MESH = pl.DeviceIdType.MESH
NX, NY, NZ = 4, 4, 16
BF = jnp.bfloat16
F32 = jnp.float32
DIRECT = (6, 10, 8, 4, 12, 3, 13, 2, 14, 1, 15)
RELAYED = (5, 7, 9, 11)


CHILDREN = {7: (6, 5), 0: (2,), 6: (4,), 2: (3,)}
ADDERS = (((0, 3, 0), (0, 2, 0), (1, 1, 1), (3, 1, 0)), ((0, 3, 1), (0, 2, 1), (0, 4, 1), (2, 1, 0)))


ORDER = ((3, 1, 2, 0), (1, 0, 2, 3))


def place(e):
    return e // 2, e % 2, e // 4


def node_place(e):
    x, z, core = place(e)
    return x, z, 1 - core


def comm_kernel(
    pend, panel_in, scale_in, linv_in, out, scaled,
    panel, scale, linv, pown, xin, part, fan, sol, pcol, acc, sums, terms, taken, oblk,
    ready, ld, lp, xs, xr, ps, pr, as_, ar, ls, lr, qs, qr, rs, us, bs, br, ds_, dr, es, er, zs, zr_, ts, fs, fr,
):
    row, col = lax.axis_index("row"), lax.axis_index("col")
    x, z = row // NZ, row % NZ
    y, h = col // 2, col % 2
    other = 2 * y + (1 - h)
    mine = h == x // 2
    lead_chip = z < 2
    lead = jnp.logical_and(lead_chip, mine)
    my_j = jnp.where(z == 0, 0, 1)
    my_e = jnp.where(lead, 2 * x + my_j, -1)
    source = [row == k for k in range(2)]
    my_node = jnp.where(jnp.logical_and(lead_chip, jnp.logical_not(mine)), 2 * x + my_j, -1)
    my_add = jnp.int32(-1)
    add_core = jnp.int32(0)
    for hs in range(2):
        for i, (ax, az, ac) in enumerate(ADDERS[hs]):
            here = jnp.logical_and(row == ax * NZ + az, h == ac)
            my_add = jnp.where(here, i, my_add)
            add_core = jnp.where(here, hs, add_core)

    def add_place(i):
        a, b = ADDERS[0][i], ADDERS[1][i]
        return [jnp.where(h == 0, p, q) for p, q in zip(a, b)]

    adder = my_add >= 0
    before = jnp.logical_or(my_node == 0, my_node == 6)
    behind = jnp.logical_or(my_e == 1, my_e == 7)
    my_node = jnp.where(my_node == 1, -1, my_node)
    my_rows = pl.ds(pl.multiple_of(y * 256, 256), 256)

    def dev(xx, zz, cc):
        return (xx * NZ + zz, cc)

    def solver(e, yy):
        ex, ez, eh = place(e)
        return dev(ex, ez, 2 * yy + eh)

    is_source = jnp.logical_or(source[0], source[1])

    def node(n, yy):
        nx, nz, nh = node_place(n)
        return dev(nx, nz, 2 * yy + nh)

    def lanes(i):
        return pl.ds(pl.multiple_of(i * 128, 128), 128)

    def load(n):
        src, dst = ((panel_in, panel), (scale_in, scale), (linv_in, linv.at[:, pl.ds(0, 128)]))[n]
        return pltpu.make_async_copy(src, dst, ld.at[n])

    def load_own(i):
        return pltpu.make_async_copy(pend.at[:, lanes(4 * h + i)], pown.at[i], lp.at[i])

    load(0).start()
    load(1).start()

    @pl.when(lead)
    def _():
        load(2).start()

    @pl.when(is_source)
    def _():
        for i in range(4):
            load_own(i).start()

    bar = pltpu.get_barrier_semaphore()

    def hello(target):
        pl.semaphore_signal(bar, inc=1, device_id=target, device_id_type=MESH)

    def both(p, q):
        return jnp.logical_and(p, q)

    def no(p):
        return jnp.logical_not(p)

    for yd in range(NY):
        sy = (y + yd) % NY
        if yd:
            @pl.when(lead)
            def _():
                hello((row, 2 * sy + h))
        heads = both(lead, no(behind))

        @pl.when(both(heads, no(source[0])) if yd == 0 else heads)
        def _():
            hello((0, 2 * sy + h))

        @pl.when(before)
        def _():
            hello((0, 2 * sy + 1 - h))

        @pl.when(adder)
        def _():
            hello((1, 2 * sy + add_core))

    for parent, children in CHILDREN.items():
        for child in children:
            @pl.when(my_node == child)
            def _():
                hello(node(parent, y))
    @pl.when(behind)
    def _():
        hello(dev(x, 0, other))

    @pl.when(jnp.logical_or(my_node == 0, my_node == 7))
    def _():
        for hh in range(2):
            hello((1, 2 * y + hh))
    for i in range(4):
        ax, az, ac = add_place(i)
        for yd in range(NY):
            @pl.when(both(both(lead, my_e % 4 == i), y >= yd))
            def _():
                hello(dev(ax, az, 2 * (y - yd) + ac))
    hello((row, other))
    lead_col = 2 * y + x // 2
    line_z = (0, 1)
    away = [(z - lz + NZ) % NZ for lz in line_z]

    def among(v, values):
        hit = v == values[0]
        for w in values[1:]:
            hit = jnp.logical_or(hit, v == w)
        return hit

    direct = [among(a, DIRECT) for a in away]
    relayed = [among(a, RELAYED) for a in away]
    relays = [among(a, (6, 10)) for a in away]
    my_leads = jnp.where(direct[0], 1, 0) + jnp.where(direct[1], 1, 0)
    for j in range(2):
        @pl.when(relayed[j])
        def _():
            step = jnp.where(jnp.logical_or(away[j] == 7, away[j] == 11), NZ - 1, 1)
            hello(dev(x, (z + step) % NZ, col))
        my_leads += jnp.where(relays[j], 2, 0)

    @pl.when(lead)
    def _():
        for d in DIRECT:
            for hh in range(2):
                hello(dev(x, (z + d) % NZ, 2 * y + hh))
    for d in range(1, NX):
        hello(dev((x + d) % NX, z, col))
    expect = 1 + NX - 1 + my_leads + jnp.where(lead, NY - 1, 0)
    expect += jnp.where(source[0], jnp.where(h == 0, 4 * NY - 1, 4 * NY), 0)
    expect += jnp.where(source[1], 4 * NY + 2, 0)
    expect += jnp.where(adder, NY - y, 0) + jnp.where(before, 1, 0)
    for parent, children in CHILDREN.items():
        expect += jnp.where(my_node == parent, len(children), 0)

    def scale_panel():
        load(0).wait()
        load(1).wait()
        for k in range(2):
            active = jnp.where(row > k, 1.0, 0.0)

            def scale_rows(r, c):
                rows = pl.ds(pl.multiple_of(r * 256, 256), 256)
                s = jnp.broadcast_to(scale[k : k + 1, rows] * active, (128, 256)).T
                scaled[rows, k * 128 : (k + 1) * 128] = (panel[rows, k, :].astype(F32) * s).astype(BF)
                return c
            lax.fori_loop(0, 4, scale_rows, 0)

    @pl.when(source[1])
    def _():
        scale_panel()

    pl.semaphore_wait(bar, expect)

    for j in range(2):
        @pl.when(direct[j])
        def _():
            pl.semaphore_signal(
                ready, inc=1, device_id=dev(x, line_z[j], lead_col), device_id_type=MESH)

    def remote(src, dst, send, recv, target):
        return pltpu.make_async_remote_copy(
            src, dst, send, recv, device_id=target, device_id_type=MESH)

    def linv_copy(k):
        return remote(linv_in.at[k], linv.at[k, pl.ds(128, 128)], ls.at[k], lr.at[k], (row, other))

    def swap_copy(i):
        return remote(pend.at[:, lanes(4 * (1 - h) + i)], xin.at[i], xs.at[i], xr.at[i], (row, other))

    def scatter_copy(k, i, yd):
        tx, tz, core = 2 * h + i // 2, (0, h, 0, 1 - h)[i], (h, 1, h, 0)[i]
        if k == 1:
            tx, tz, core = add_place(i)
        ty = (y + yd) % NY
        rows = pl.ds(pl.multiple_of(ty * 256, 256), 256)
        return remote(xin.at[i, rows], part.at[k, yd], ps.at[i, yd], pr.at[k, yd],
                      dev(tx, tz, 2 * ty + core))

    def before_copy():
        return remote(acc, fan.at[0, my_rows], bs, br, dev(x, 1, other))

    def before_wait():
        return remote(acc, fan.at[0, my_rows], bs, br, dev(x, 0, other))

    def panel_block(q):
        return pcol.at[pl.ds((q % 4) * 256, 256), pl.ds((q // 4) * 128, 128)]

    def panel_copy(t, r):
        rows = pl.ds(r * 256, 256)
        target = (node(0, y), (row, other), node(7, y))[t]
        return remote(scaled.at[rows, pl.ds(0, 128)], pcol.at[rows, lanes(h)],
                      qs.at[t, r], qr.at[4 * h + r], target)

    def panel_wait(q):
        return remote(panel_block(q), panel_block(q), qs.at[0, 0], qr.at[q], (row, other))

    def relay_copy(child, n, q):
        return remote(panel_block(q), panel_block(q), rs.at[n, q], qr.at[q], node(child, y))

    def mate_copy(q):
        return remote(panel_block(q), panel_block(q), us.at[q], qr.at[q], (row, other))

    def sums_copy(i, yd):
        tz = i % 2
        return remote(acc, sums.at[my_rows], ds_.at[yd], dr.at[y],
                      dev(2 * add_core + i // 2, tz, 2 * (y + yd) + add_core))

    def sums_wait(sy):
        rows = sums.at[pl.ds(sy * 256, 256)]
        return remote(rows, rows, ds_.at[0], dr.at[sy], (row, other))

    def terms_copy(t):
        rows = pl.ds(0, (t + 1) * 256)
        return remote(terms.at[rows], taken.at[y, rows], es.at[t], er.at[y], (row, 2 * t + h))

    def terms_wait(t, sy):
        rows = taken.at[sy, pl.ds(0, (t + 1) * 256)]
        return remote(rows, rows, es.at[t], er.at[sy], (row, other))

    def gather_copy(buf, n, yd):
        return remote(buf.at[my_rows], buf.at[my_rows], as_.at[n, yd - 1], ar.at[n, yd - 1],
                      (row, 2 * ((y + yd) % NY) + h))

    def piece(k, xx, j):
        return out.at[k, :, lanes(2 * xx + j)]

    def line_copy(k, j, d, same):
        return remote(piece(k, x, j) if same else oblk.at[k], piece(k, x, j),
                      zs.at[k, d, 0 if same else 1], zr_.at[k, j],
                      dev(x, (z + d) % NZ, col if same else other))

    def pass_copy(k, j, n):
        return remote(piece(k, x, j), piece(k, x, j), ts.at[k, n], zr_.at[k, j],
                      dev(x, (z + (1, NZ - 1)[n]) % NZ, col))

    def spread_copy(k, j, d):
        return remote(piece(k, x, j), piece(k, x, j), fs.at[k, j, d - 1], fr.at[k, j, d - 1],
                      dev((x + d) % NX, z, col))

    def spread_wait(k, j, d):
        fx = (x + NX - d) % NX
        return remote(piece(k, fx, j), piece(k, fx, j), fs.at[k, j, d - 1], fr.at[k, j, d - 1],
                      dev(fx, z, col))

    def spread(k):
        for j in range(2):
            @pl.when(no(both(lead, my_j == j)))
            def _():
                line_copy(k, j, 0, False).wait_recv()

            @pl.when(relays[j])
            def _():
                for n in range(2):
                    pass_copy(k, j, n).start()
            for d in (2, 1, 3):
                spread_copy(k, j, d).start()

    def unless_local(k, i, yd, action, local=None):
        if not (k == 0 and i == 0 and yd == 0):
            action()
        else:
            pl.when(h != 0)(action)
            if local:
                pl.when(h == 0)(local)

    @pl.when(both(lead_chip, no(mine)))
    def _():
        for k in range(2):
            linv_copy(k).start()

    @pl.when(is_source)
    def _():
        for k in range(2):
            @pl.when(source[k])
            def _():
                for i in ORDER[k]:
                    swap_copy(i).start()

    @pl.when(source[1])
    def _():
        for r in range(4):
            panel_copy(0, r).start()
            panel_copy(2, r).start()

        @pl.when(h == 0)
        def _():
            pcol[:, 0:128] = scaled[:, 0:128]

        @pl.when(h == 1)
        def _():
            for r in range(4):
                panel_copy(1, r).start()

    for k in range(2):
        @pl.when(source[k])
        def _():
            for i in ORDER[k]:
                load_own(i).wait()
                swap_copy(i).wait_recv()

                def add(r, c):
                    rows = pl.ds(pl.multiple_of(r * 256, 256), 256)
                    xin[i, rows] = (pown[i, rows].astype(F32) + xin[i, rows].astype(F32)).astype(BF)
                    return c
                lax.fori_loop(0, 4, add, 0)

                def keep():
                    part[k, 0] = xin[i, my_rows]
                for yd in (2, 1, 3, 0):
                    unless_local(k, i, yd, lambda: scatter_copy(k, i, yd).start(), keep)

    def reduced(k):
        if k == 1:
            scatter_copy(k, 0, 0).wait_recv()
        else:
            @pl.when(my_e != 0)
            def _():
                scatter_copy(k, 0, 0).wait_recv()
        for yd in range(1, NY):
            scatter_copy(k, 0, yd).wait_recv()
        total = part[k, 0].astype(F32)
        for yd in range(1, NY):
            total += part[k, yd].astype(F32)
        return total

    def gather_start(buf, n):
        for yd in (2, 1, 3):
            gather_copy(buf, n, yd).start()

    def gather_wait(buf, n):
        for yd in range(1, NY):
            gather_copy(buf, n, yd).wait_recv()

    def solve(k, depth):
        blocks = jnp.dot(linv[k, :, :depth], fan[k, :depth], preferred_element_type=F32).astype(BF)
        oblk[k] = blocks[128:]
        out[k, :, lanes(2 * x + my_j)] = blocks[:128]
        return blocks

    def line_start(k):
        for j in range(2):
            @pl.when(my_j == j)
            def _():
                for d in DIRECT:
                    line_copy(k, j, d, False).start()
                    line_copy(k, j, d, True).start()
                line_copy(k, j, 0, False).start()

    def add_up():
        @pl.when(adder)
        def _():
            acc[...] = reduced(1).astype(BF)
            for i in range(4):
                for yd in (2, 1, 3, 0):
                    @pl.when(both(my_add == i, y + yd < NY))
                    def _():
                        sums_copy(i, yd).start()

    @pl.when(before)
    def _():
        acc[...] = reduced(0).astype(BF)
        before_copy().start()

    @pl.when(my_node >= 0)
    def _():
        for c in (0, 4, 1, 5, 2, 6, 3, 7):
            panel_wait(c).wait_recv()
            for parent, children in CHILDREN.items():
                @pl.when(my_node == parent)
                def _():
                    for n, child in enumerate(children):
                        relay_copy(child, n, c).start()

            mate_copy(c).start()

    @pl.when(lead)
    def _():
        @pl.when(behind)
        def _():
            before_wait().wait_recv()

        @pl.when(no(behind))
        def _():
            fan[0, my_rows] = reduced(0).astype(BF)
        gather_start(fan.at[0], 0)
        for k in range(2):
            linv_copy(k).wait_recv()
        load(2).wait()
        gather_wait(fan.at[0], 0)
        blocks = solve(0, fan.shape[1])
        sol[pl.ds(pl.multiple_of(h * 128, 128), 128)] = blocks[:128]
        sol[pl.ds(pl.multiple_of((1 - h) * 128, 128), 128)] = blocks[128:]
        for q in range(8):
            if q < 4:
                @pl.when(my_e != 1)
                def _():
                    panel_wait(q).wait_recv()
            else:
                panel_wait(q).wait_recv()
        terms[...] = jnp.dot(pcol[...], sol[...], preferred_element_type=F32).astype(BF)
        for t in (3, 2, 1, 0):
            @pl.when(y != t)
            def _():
                terms_copy(t).start()
        pl.semaphore_wait(ready, 2 * len(DIRECT))
        line_start(0)
        spread(0)
        for t in range(NY):
            @pl.when(y == t)
            def _():
                depth = (t + 1) * 256
                for sy in range(t + 1):
                    sums_wait(sy).wait_recv()
                total = sums[:depth].astype(F32) - terms[:depth].astype(F32)
                for sy in range(NY):
                    if sy != t:
                        terms_wait(t, sy).wait_recv()
                        total -= taken[sy, :depth].astype(F32)
                fan[1, :depth] = total.astype(BF)
                solve(1, depth)
        line_start(1)

    @pl.when(no(lead))
    def _():
        add_up()

        @pl.when(no(source[1]))
        def _():
            scale_panel()
        spread(0)

    @pl.when(both(lead, no(source[1])))
    def _():
        scale_panel()
    spread(1)

    for k in range(2):
        for j in range(2):
            for d in range(1, NX):
                spread_wait(k, j, d).wait_recv()

    for k in range(2):
        for j in range(2):
            for d in range(1, NX):
                spread_copy(k, j, d).wait_send()

            @pl.when(relays[j])
            def _():
                for n in range(2):
                    pass_copy(k, j, n).wait_send()

    @pl.when(both(lead_chip, no(mine)))
    def _():
        for k in range(2):
            linv_copy(k).wait_send()

    for k in range(2):
        @pl.when(source[k])
        def _():
            for i in range(4):
                swap_copy(i).wait_send()
                for yd in range(NY):
                    unless_local(k, i, yd, lambda: scatter_copy(k, i, yd).wait_send())

    @pl.when(source[1])
    def _():
        for r in range(4):
            panel_copy(0, r).wait_send()
            panel_copy(2, r).wait_send()

        @pl.when(h == 1)
        def _():
            for r in range(4):
                panel_copy(1, r).wait_send()

    @pl.when(lead)
    def _():
        for yd in range(1, NY):
            gather_copy(fan.at[0], 0, yd).wait_send()
        for t in range(NY):
            @pl.when(y != t)
            def _():
                terms_copy(t).wait_send()
        for k in range(2):
            for d in DIRECT:
                line_copy(k, 0, d, False).wait_send()
                line_copy(k, 0, d, True).wait_send()
            line_copy(k, 0, 0, False).wait_send()
    @pl.when(before)
    def _():
        before_copy().wait_send()

    @pl.when(adder)
    def _():
        for yd in range(NY):
            @pl.when(y + yd < NY)
            def _():
                sums_copy(0, yd).wait_send()

    @pl.when(my_node >= 0)
    def _():
        for c in range(8):
            for parent, children in CHILDREN.items():
                @pl.when(my_node == parent)
                def _():
                    for n, child in enumerate(children):
                        relay_copy(child, n, c).wait_send()

            mate_copy(c).wait_send()


def update_kernel(pend, scaled, solved, out, solved_out, done, sem):
    tiles = done.shape[0]
    size = done.shape[2]
    last = pltpu.make_async_copy(solved, solved_out, sem.at[tiles])
    last.start()

    def store(i):
        return pltpu.make_async_copy(
            done.at[i], out.at[:, pl.ds(pl.multiple_of(i * size, size), size)], sem.at[i])

    def tile(i, c):
        cols = pl.ds(pl.multiple_of(i * size, size), size)
        term = jnp.dot(scaled[...], solved[:, cols], preferred_element_type=F32)
        done[i] = (pend[:, cols].astype(F32) - term).astype(BF)
        store(i).start()
        return c
    lax.fori_loop(0, tiles, tile, 0)
    for i in range(tiles):
        store(i).wait()
    last.wait()


def body(pending, panel, panel_scale, inverse_blocks):
    rows, _, cols = pending.shape
    current = pending.reshape(rows, cols)
    vmem = pl.BlockSpec(memory_space=pltpu.VMEM)
    hbm = pl.BlockSpec(memory_space=pltpu.HBM)
    dma = pltpu.SemaphoreType.DMA
    solved, scaled = pl.pallas_call(
        comm_kernel,
        out_shape=(jax.ShapeDtypeStruct((2, 128, cols), BF), jax.ShapeDtypeStruct((rows, 256), BF)),
        in_specs=[hbm] * 4,
        out_specs=(vmem, vmem),
        scratch_shapes=[
            pltpu.VMEM((rows, 2, 128), BF),
            pltpu.VMEM((2, rows), F32),
            pltpu.VMEM((2, 256, rows), BF),
            pltpu.VMEM((4, rows, 128), BF),
            pltpu.VMEM((4, rows, 128), BF),
            pltpu.VMEM((2, NY, 256, 128), BF),
            pltpu.VMEM((2, rows, 128), BF),
            pltpu.VMEM((256, 128), BF),
            pltpu.VMEM((rows, 256), BF),
            pltpu.VMEM((256, 128), BF),
            pltpu.VMEM((rows, 128), BF),
            pltpu.VMEM((rows, 128), BF),
            pltpu.VMEM((NY, rows, 128), BF),
            pltpu.VMEM((2, 128, 128), BF),
            pltpu.SemaphoreType.REGULAR, dma((3,)), dma((4,)),
            dma((4,)), dma((4,)), dma((4, NY)), dma((2, NY)),
            dma((1, NY - 1)), dma((1, NY - 1)), dma((2,)), dma((2,)),
            dma((3, 4)), dma((8,)), dma((2, 8)), dma((8,)), dma, dma, dma((NY,)), dma((NY,)),
            dma((NY,)), dma((NY,)),
            dma((2, NZ, 2)), dma((2, 2)), dma((2, 2)), dma((2, 2, NX - 1)), dma((2, 2, NX - 1)),
        ],
        compiler_params=pltpu.CompilerParams(
            collective_id=0, has_side_effects=True, vmem_limit_bytes=32 << 20),
        name="substitute",
    )(*(pltpu.with_memory_space_constraint(v, pltpu.HBM)
        for v in (current, panel, panel_scale.T, inverse_blocks)))
    remaining, solved = pl.pallas_call(
        update_kernel,
        out_shape=(jax.ShapeDtypeStruct((rows, cols), BF), jax.ShapeDtypeStruct((256, cols), BF)),
        in_specs=[vmem] * 3,
        out_specs=(hbm, hbm),
        scratch_shapes=[pltpu.VMEM((4, rows, cols // 4), BF), dma((5,))],
        compiler_params=pltpu.CompilerParams(vmem_limit_bytes=32 << 20),
        name="update",
    )(current, scaled, solved.reshape(256, cols))
    return remaining[:, None, :], solved.reshape(2, 128, cols)


def solution(mesh):
    placed = (P("row", "col", None), P("row", None, "col"), P("row", None), P(None, "col", None))
    return jax.shard_map(
        body,
        mesh=mesh,
        in_specs=placed,
        out_specs=(P("row", "col", None), P(None, "col", None)),
        check_vma=False,
    )
```

```python
import functools

import jax
import jax.numpy as jnp
from jax import lax
from jax.experimental import pallas as pl
from jax.experimental.pallas import tpu as pltpu
from jax.sharding import PartitionSpec as P

MESH = pl.DeviceIdType.MESH
NX, NY, NZ = 4, 4, 16
BF = jnp.bfloat16
F32 = jnp.float32
DIRECT = (6, 10, 8, 4, 12, 3, 13, 2, 14, 1, 15)
RELAYED = (5, 7, 9, 11)


CHILDREN = {7: (6, 5), 0: (2,), 6: (4,), 2: (3,)}
ADDERS = (((1, 2, 0), (0, 2, 0), (3, 1, 0), (1, 1, 1)), ((3, 2, 1), (0, 2, 1), (1, 2, 1), (2, 1, 0)))


ORDER = ((3, 1, 2, 0), (0, 2, 1, 3))


def place(e):
    return e // 2, e % 2, e // 4


def node_place(e):
    x, z, core = place(e)
    return x, z, 1 - core


def comm_kernel(
    pend, panel_in, scale_in, linv_in, out, scaled,
    panel, scale, linv, pown, xin, part, fan, sol, pcol, acc, sums, terms, taken, oblk,
    ready, ld, lp, xs, xr, ps, pr, as_, ar, ls, lr, qs, qr, rs, us, bs, br, ds_, dr, es, er, zs, zr_, ts, fs, fr,
):
    row, col = lax.axis_index("row"), lax.axis_index("col")
    x, z = row // NZ, row % NZ
    y, h = col // 2, col % 2
    other = 2 * y + (1 - h)
    mine = h == x // 2
    lead_chip = z < 2
    lead = jnp.logical_and(lead_chip, mine)
    my_j = jnp.where(z == 0, 0, 1)
    my_e = jnp.where(lead, 2 * x + my_j, -1)
    source = [row == k for k in range(2)]
    my_node = jnp.where(jnp.logical_and(lead_chip, jnp.logical_not(mine)), 2 * x + my_j, -1)
    my_add = jnp.int32(-1)
    add_core = jnp.int32(0)
    for hs in range(2):
        for i, (ax, az, ac) in enumerate(ADDERS[hs]):
            here = jnp.logical_and(row == ax * NZ + az, h == ac)
            my_add = jnp.where(here, i, my_add)
            add_core = jnp.where(here, hs, add_core)

    def add_place(i):
        a, b = ADDERS[0][i], ADDERS[1][i]
        return [jnp.where(h == 0, p, q) for p, q in zip(a, b)]

    adder = my_add >= 0
    before = jnp.logical_or(my_node == 0, my_node == 6)
    behind = jnp.logical_or(my_e == 1, my_e == 7)
    my_node = jnp.where(my_node == 1, -1, my_node)
    my_rows = pl.ds(pl.multiple_of(y * 256, 256), 256)

    def dev(xx, zz, cc):
        return (xx * NZ + zz, cc)

    def solver(e, yy):
        ex, ez, eh = place(e)
        return dev(ex, ez, 2 * yy + eh)

    is_source = jnp.logical_or(source[0], source[1])

    def node(n, yy):
        nx, nz, nh = node_place(n)
        return dev(nx, nz, 2 * yy + nh)

    def lanes(i):
        return pl.ds(pl.multiple_of(i * 128, 128), 128)

    def load(n):
        src, dst = ((panel_in, panel), (scale_in, scale), (linv_in, linv.at[:, pl.ds(0, 128)]))[n]
        return pltpu.make_async_copy(src, dst, ld.at[n])

    def load_own(i):
        return pltpu.make_async_copy(pend.at[:, lanes(4 * h + i)], pown.at[i], lp.at[i])

    load(0).start()
    load(1).start()

    @pl.when(lead)
    def _():
        load(2).start()

    @pl.when(is_source)
    def _():
        for i in range(4):
            load_own(i).start()

    bar = pltpu.get_barrier_semaphore()

    def hello(target):
        pl.semaphore_signal(bar, inc=1, device_id=target, device_id_type=MESH)

    def both(p, q):
        return jnp.logical_and(p, q)

    def no(p):
        return jnp.logical_not(p)

    for yd in range(NY):
        sy = (y + yd) % NY
        if yd:
            @pl.when(lead)
            def _():
                hello((row, 2 * sy + h))
        heads = both(lead, no(behind))

        @pl.when(both(heads, no(source[0])) if yd == 0 else heads)
        def _():
            hello((0, 2 * sy + h))

        @pl.when(before)
        def _():
            hello((0, 2 * sy + 1 - h))

        @pl.when(adder)
        def _():
            hello((1, 2 * sy + add_core))

    for parent, children in CHILDREN.items():
        for child in children:
            @pl.when(my_node == child)
            def _():
                hello(node(parent, y))
    @pl.when(behind)
    def _():
        hello(dev(x, 0, other))

    @pl.when(jnp.logical_or(my_node == 0, my_node == 7))
    def _():
        for hh in range(2):
            hello((1, 2 * y + hh))
    for i in range(4):
        ax, az, ac = add_place(i)
        for yd in range(NY):
            @pl.when(both(both(lead, my_e % 4 == i), y >= yd))
            def _():
                hello(dev(ax, az, 2 * (y - yd) + ac))
    hello((row, other))
    lead_col = 2 * y + x // 2
    line_z = (0, 1)
    away = [(z - lz + NZ) % NZ for lz in line_z]

    def among(v, values):
        hit = v == values[0]
        for w in values[1:]:
            hit = jnp.logical_or(hit, v == w)
        return hit

    direct = [among(a, DIRECT) for a in away]
    relayed = [among(a, RELAYED) for a in away]
    relays = [among(a, (6, 10)) for a in away]
    my_leads = jnp.where(direct[0], 1, 0) + jnp.where(direct[1], 1, 0)
    for j in range(2):
        @pl.when(relayed[j])
        def _():
            step = jnp.where(jnp.logical_or(away[j] == 7, away[j] == 11), NZ - 1, 1)
            hello(dev(x, (z + step) % NZ, col))
        my_leads += jnp.where(relays[j], 2, 0)

    @pl.when(lead)
    def _():
        for d in DIRECT:
            for hh in range(2):
                hello(dev(x, (z + d) % NZ, 2 * y + hh))
    for d in range(1, NX):
        hello(dev((x + d) % NX, z, col))
    expect = 1 + NX - 1 + my_leads + jnp.where(lead, NY - 1, 0)
    expect += jnp.where(source[0], jnp.where(h == 0, 4 * NY - 1, 4 * NY), 0)
    expect += jnp.where(source[1], 4 * NY + 2, 0)
    expect += jnp.where(adder, NY - y, 0) + jnp.where(before, 1, 0)
    for parent, children in CHILDREN.items():
        expect += jnp.where(my_node == parent, len(children), 0)

    def scale_panel():
        load(0).wait()
        load(1).wait()
        for k in range(2):
            active = jnp.where(row > k, 1.0, 0.0)

            def scale_rows(r, c):
                rows = pl.ds(pl.multiple_of(r * 256, 256), 256)
                s = jnp.broadcast_to(scale[k : k + 1, rows] * active, (128, 256)).T
                scaled[rows, k * 128 : (k + 1) * 128] = (panel[rows, k, :].astype(F32) * s).astype(BF)
                return c
            lax.fori_loop(0, 4, scale_rows, 0)

    @pl.when(source[1])
    def _():
        scale_panel()

    pl.semaphore_wait(bar, expect)

    for j in range(2):
        @pl.when(direct[j])
        def _():
            pl.semaphore_signal(
                ready, inc=1, device_id=dev(x, line_z[j], lead_col), device_id_type=MESH)

    def remote(src, dst, send, recv, target):
        return pltpu.make_async_remote_copy(
            src, dst, send, recv, device_id=target, device_id_type=MESH)

    def linv_copy(k):
        return remote(linv_in.at[k], linv.at[k, pl.ds(128, 128)], ls.at[k], lr.at[k], (row, other))

    def swap_copy(i):
        return remote(pend.at[:, lanes(4 * (1 - h) + i)], xin.at[i], xs.at[i], xr.at[i], (row, other))

    def scatter_copy(k, i, yd):
        tx, tz, core = 2 * h + i // 2, (0, h, 0, 1 - h)[i], (h, 1, h, 0)[i]
        if k == 1:
            tx, tz, core = add_place(i)
        ty = (y + yd) % NY
        rows = pl.ds(pl.multiple_of(ty * 256, 256), 256)
        return remote(xin.at[i, rows], part.at[k, yd], ps.at[i, yd], pr.at[k, yd],
                      dev(tx, tz, 2 * ty + core))

    def before_copy():
        return remote(acc, fan.at[0, my_rows], bs, br, dev(x, 1, other))

    def before_wait():
        return remote(acc, fan.at[0, my_rows], bs, br, dev(x, 0, other))

    def panel_block(q):
        return pcol.at[pl.ds((q % 4) * 256, 256), pl.ds((q // 4) * 128, 128)]

    def panel_copy(t, r):
        rows = pl.ds(r * 256, 256)
        target = (node(0, y), (row, other), node(7, y))[t]
        return remote(scaled.at[rows, pl.ds(0, 128)], pcol.at[rows, lanes(h)],
                      qs.at[t, r], qr.at[4 * h + r], target)

    def panel_wait(q):
        return remote(panel_block(q), panel_block(q), qs.at[0, 0], qr.at[q], (row, other))

    def relay_copy(child, n, q):
        return remote(panel_block(q), panel_block(q), rs.at[n, q], qr.at[q], node(child, y))

    def mate_copy(q):
        return remote(panel_block(q), panel_block(q), us.at[q], qr.at[q], (row, other))

    def sums_copy(i, yd):
        tz = i % 2
        return remote(acc, sums.at[my_rows], ds_.at[yd], dr.at[y],
                      dev(2 * add_core + i // 2, tz, 2 * (y + yd) + add_core))

    def sums_wait(sy):
        rows = sums.at[pl.ds(sy * 256, 256)]
        return remote(rows, rows, ds_.at[0], dr.at[sy], (row, other))

    def terms_copy(t):
        rows = pl.ds(0, (t + 1) * 256)
        return remote(terms.at[rows], taken.at[y, rows], es.at[t], er.at[y], (row, 2 * t + h))

    def terms_wait(t, sy):
        rows = taken.at[sy, pl.ds(0, (t + 1) * 256)]
        return remote(rows, rows, es.at[t], er.at[sy], (row, other))

    def gather_copy(buf, n, yd):
        return remote(buf.at[my_rows], buf.at[my_rows], as_.at[n, yd - 1], ar.at[n, yd - 1],
                      (row, 2 * ((y + yd) % NY) + h))

    def piece(k, xx, j):
        return out.at[k, :, lanes(2 * xx + j)]

    def line_copy(k, j, d, same):
        return remote(piece(k, x, j) if same else oblk.at[k], piece(k, x, j),
                      zs.at[k, d, 0 if same else 1], zr_.at[k, j],
                      dev(x, (z + d) % NZ, col if same else other))

    def pass_copy(k, j, n):
        return remote(piece(k, x, j), piece(k, x, j), ts.at[k, n], zr_.at[k, j],
                      dev(x, (z + (1, NZ - 1)[n]) % NZ, col))

    def spread_copy(k, j, d):
        return remote(piece(k, x, j), piece(k, x, j), fs.at[k, j, d - 1], fr.at[k, j, d - 1],
                      dev((x + d) % NX, z, col))

    def spread_wait(k, j, d):
        fx = (x + NX - d) % NX
        return remote(piece(k, fx, j), piece(k, fx, j), fs.at[k, j, d - 1], fr.at[k, j, d - 1],
                      dev(fx, z, col))

    def spread(k):
        for j in range(2):
            @pl.when(no(both(lead, my_j == j)))
            def _():
                line_copy(k, j, 0, False).wait_recv()

            @pl.when(relays[j])
            def _():
                for n in range(2):
                    pass_copy(k, j, n).start()
            for d in (2, 1, 3):
                spread_copy(k, j, d).start()

    def unless_local(k, i, yd, action, local=None):
        if not (k == 0 and i == 0 and yd == 0):
            action()
        else:
            pl.when(h != 0)(action)
            if local:
                pl.when(h == 0)(local)

    @pl.when(both(lead_chip, no(mine)))
    def _():
        for k in range(2):
            linv_copy(k).start()

    @pl.when(is_source)
    def _():
        for k in range(2):
            @pl.when(source[k])
            def _():
                for i in ORDER[k]:
                    swap_copy(i).start()

    @pl.when(source[1])
    def _():
        for r in range(4):
            panel_copy(0, r).start()
            panel_copy(2, r).start()

        @pl.when(h == 0)
        def _():
            pcol[:, 0:128] = scaled[:, 0:128]

        @pl.when(h == 1)
        def _():
            for r in range(4):
                panel_copy(1, r).start()

    for k in range(2):
        @pl.when(source[k])
        def _():
            for i in ORDER[k]:
                load_own(i).wait()
                swap_copy(i).wait_recv()

                def add(r, c):
                    rows = pl.ds(pl.multiple_of(r * 256, 256), 256)
                    xin[i, rows] = (pown[i, rows].astype(F32) + xin[i, rows].astype(F32)).astype(BF)
                    return c
                lax.fori_loop(0, 4, add, 0)

                def keep():
                    part[k, 0] = xin[i, my_rows]
                for yd in (2, 1, 3, 0):
                    unless_local(k, i, yd, lambda: scatter_copy(k, i, yd).start(), keep)

    def reduced(k):
        if k == 1:
            scatter_copy(k, 0, 0).wait_recv()
        else:
            @pl.when(my_e != 0)
            def _():
                scatter_copy(k, 0, 0).wait_recv()
        for yd in range(1, NY):
            scatter_copy(k, 0, yd).wait_recv()
        total = part[k, 0].astype(F32)
        for yd in range(1, NY):
            total += part[k, yd].astype(F32)
        return total

    def gather_start(buf, n):
        for yd in (2, 1, 3):
            gather_copy(buf, n, yd).start()

    def gather_wait(buf, n):
        for yd in range(1, NY):
            gather_copy(buf, n, yd).wait_recv()

    def solve(k, depth):
        blocks = jnp.dot(linv[k, :, :depth], fan[k, :depth], preferred_element_type=F32).astype(BF)
        oblk[k] = blocks[128:]
        out[k, :, lanes(2 * x + my_j)] = blocks[:128]
        return blocks

    def line_start(k):
        for j in range(2):
            @pl.when(my_j == j)
            def _():
                for d in DIRECT:
                    line_copy(k, j, d, False).start()
                    line_copy(k, j, d, True).start()
                line_copy(k, j, 0, False).start()

    def add_up(which):
        @pl.when(both(adder, which))
        def _():
            acc[...] = reduced(1).astype(BF)
            for i in range(4):
                for yd in (2, 1, 3, 0):
                    @pl.when(both(my_add == i, y + yd < NY))
                    def _():
                        sums_copy(i, yd).start()

    @pl.when(before)
    def _():
        acc[...] = reduced(0).astype(BF)
        before_copy().start()

    add_up(my_node != 7)

    @pl.when(my_node >= 0)
    def _():
        for c in (0, 4, 1, 5, 2, 6, 3, 7):
            panel_wait(c).wait_recv()
            for parent, children in CHILDREN.items():
                @pl.when(my_node == parent)
                def _():
                    for n, child in enumerate(children):
                        relay_copy(child, n, c).start()

            mate_copy(c).start()

    @pl.when(lead)
    def _():
        @pl.when(behind)
        def _():
            before_wait().wait_recv()

        @pl.when(no(behind))
        def _():
            fan[0, my_rows] = reduced(0).astype(BF)
        gather_start(fan.at[0], 0)
        for k in range(2):
            linv_copy(k).wait_recv()
        load(2).wait()
        gather_wait(fan.at[0], 0)
        blocks = solve(0, fan.shape[1])
        sol[pl.ds(pl.multiple_of(h * 128, 128), 128)] = blocks[:128]
        sol[pl.ds(pl.multiple_of((1 - h) * 128, 128), 128)] = blocks[128:]
        for q in range(8):
            if q < 4:
                @pl.when(my_e != 1)
                def _():
                    panel_wait(q).wait_recv()
            else:
                panel_wait(q).wait_recv()
        terms[...] = jnp.dot(pcol[...], sol[...], preferred_element_type=F32).astype(BF)
        for t in (3, 2, 1, 0):
            @pl.when(y != t)
            def _():
                terms_copy(t).start()
        pl.semaphore_wait(ready, 2 * len(DIRECT))
        line_start(0)
        spread(0)
        for t in range(NY):
            @pl.when(y == t)
            def _():
                depth = (t + 1) * 256
                for sy in range(t + 1):
                    sums_wait(sy).wait_recv()
                total = sums[:depth].astype(F32) - terms[:depth].astype(F32)
                for sy in range(NY):
                    if sy != t:
                        terms_wait(t, sy).wait_recv()
                        total -= taken[sy, :depth].astype(F32)
                fan[1, :depth] = total.astype(BF)
                solve(1, depth)
        line_start(1)

    @pl.when(no(lead))
    def _():
        add_up(my_node == 7)

        @pl.when(no(source[1]))
        def _():
            scale_panel()
        spread(0)

    @pl.when(both(lead, no(source[1])))
    def _():
        scale_panel()
    spread(1)

    for k in range(2):
        for j in range(2):
            for d in range(1, NX):
                spread_wait(k, j, d).wait_recv()

    for k in range(2):
        for j in range(2):
            for d in range(1, NX):
                spread_copy(k, j, d).wait_send()

            @pl.when(relays[j])
            def _():
                for n in range(2):
                    pass_copy(k, j, n).wait_send()

    @pl.when(both(lead_chip, no(mine)))
    def _():
        for k in range(2):
            linv_copy(k).wait_send()

    for k in range(2):
        @pl.when(source[k])
        def _():
            for i in range(4):
                swap_copy(i).wait_send()
                for yd in range(NY):
                    unless_local(k, i, yd, lambda: scatter_copy(k, i, yd).wait_send())

    @pl.when(source[1])
    def _():
        for r in range(4):
            panel_copy(0, r).wait_send()
            panel_copy(2, r).wait_send()

        @pl.when(h == 1)
        def _():
            for r in range(4):
                panel_copy(1, r).wait_send()

    @pl.when(lead)
    def _():
        for yd in range(1, NY):
            gather_copy(fan.at[0], 0, yd).wait_send()
        for t in range(NY):
            @pl.when(y != t)
            def _():
                terms_copy(t).wait_send()
        for k in range(2):
            for d in DIRECT:
                line_copy(k, 0, d, False).wait_send()
                line_copy(k, 0, d, True).wait_send()
            line_copy(k, 0, 0, False).wait_send()
    @pl.when(before)
    def _():
        before_copy().wait_send()

    @pl.when(adder)
    def _():
        for yd in range(NY):
            @pl.when(y + yd < NY)
            def _():
                sums_copy(0, yd).wait_send()

    @pl.when(my_node >= 0)
    def _():
        for c in range(8):
            for parent, children in CHILDREN.items():
                @pl.when(my_node == parent)
                def _():
                    for n, child in enumerate(children):
                        relay_copy(child, n, c).wait_send()

            mate_copy(c).wait_send()


def update_kernel(pend, scaled, solved, out, solved_out, done, sem):
    tiles = done.shape[0]
    size = done.shape[2]
    last = pltpu.make_async_copy(solved, solved_out, sem.at[tiles])
    last.start()

    def store(i):
        return pltpu.make_async_copy(
            done.at[i], out.at[:, pl.ds(pl.multiple_of(i * size, size), size)], sem.at[i])

    def tile(i, c):
        cols = pl.ds(pl.multiple_of(i * size, size), size)
        term = jnp.dot(scaled[...], solved[:, cols], preferred_element_type=F32)
        done[i] = (pend[:, cols].astype(F32) - term).astype(BF)
        store(i).start()
        return c
    lax.fori_loop(0, tiles, tile, 0)
    for i in range(tiles):
        store(i).wait()
    last.wait()


def body(pending, panel, panel_scale, inverse_blocks):
    rows, _, cols = pending.shape
    current = pending.reshape(rows, cols)
    vmem = pl.BlockSpec(memory_space=pltpu.VMEM)
    hbm = pl.BlockSpec(memory_space=pltpu.HBM)
    dma = pltpu.SemaphoreType.DMA
    solved, scaled = pl.pallas_call(
        comm_kernel,
        out_shape=(jax.ShapeDtypeStruct((2, 128, cols), BF), jax.ShapeDtypeStruct((rows, 256), BF)),
        in_specs=[hbm] * 4,
        out_specs=(vmem, vmem),
        scratch_shapes=[
            pltpu.VMEM((rows, 2, 128), BF),
            pltpu.VMEM((2, rows), F32),
            pltpu.VMEM((2, 256, rows), BF),
            pltpu.VMEM((4, rows, 128), BF),
            pltpu.VMEM((4, rows, 128), BF),
            pltpu.VMEM((2, NY, 256, 128), BF),
            pltpu.VMEM((2, rows, 128), BF),
            pltpu.VMEM((256, 128), BF),
            pltpu.VMEM((rows, 256), BF),
            pltpu.VMEM((256, 128), BF),
            pltpu.VMEM((rows, 128), BF),
            pltpu.VMEM((rows, 128), BF),
            pltpu.VMEM((NY, rows, 128), BF),
            pltpu.VMEM((2, 128, 128), BF),
            pltpu.SemaphoreType.REGULAR, dma((3,)), dma((4,)),
            dma((4,)), dma((4,)), dma((4, NY)), dma((2, NY)),
            dma((1, NY - 1)), dma((1, NY - 1)), dma((2,)), dma((2,)),
            dma((3, 4)), dma((8,)), dma((2, 8)), dma((8,)), dma, dma, dma((NY,)), dma((NY,)),
            dma((NY,)), dma((NY,)),
            dma((2, NZ, 2)), dma((2, 2)), dma((2, 2)), dma((2, 2, NX - 1)), dma((2, 2, NX - 1)),
        ],
        compiler_params=pltpu.CompilerParams(
            collective_id=0, has_side_effects=True, vmem_limit_bytes=32 << 20),
        name="substitute",
    )(*(pltpu.with_memory_space_constraint(v, pltpu.HBM)
        for v in (current, panel, panel_scale.T, inverse_blocks)))
    remaining, solved = pl.pallas_call(
        update_kernel,
        out_shape=(jax.ShapeDtypeStruct((rows, cols), BF), jax.ShapeDtypeStruct((256, cols), BF)),
        in_specs=[vmem] * 3,
        out_specs=(hbm, hbm),
        scratch_shapes=[pltpu.VMEM((4, rows, cols // 4), BF), dma((5,))],
        compiler_params=pltpu.CompilerParams(vmem_limit_bytes=32 << 20),
        name="update",
    )(current, scaled, solved.reshape(256, cols))
    return remaining[:, None, :], solved.reshape(2, 128, cols)


def solution(mesh):
    placed = (P("row", "col", None), P("row", None, "col"), P("row", None), P(None, "col", None))
    return jax.shard_map(
        body,
        mesh=mesh,
        in_specs=placed,
        out_specs=(P("row", "col", None), P(None, "col", None)),
        check_vma=False,
    )
```

```python
import functools

import jax
import jax.numpy as jnp
from jax import lax
from jax.experimental import pallas as pl
from jax.experimental.pallas import tpu as pltpu
from jax.sharding import PartitionSpec as P

MESH = pl.DeviceIdType.MESH
NX, NY, NZ = 4, 4, 16
BF = jnp.bfloat16
F32 = jnp.float32
DIRECT = (6, 10, 4, 12, 3, 13, 2, 14, 1, 15, 8)
RELAYED = (5, 7, 9, 11)


CHILDREN = {7: (6, 5), 0: (2,), 6: (4,), 2: (3,)}
ADDERS = (((1, 2, 0), (0, 2, 0), (3, 1, 0), (1, 1, 1)), ((3, 2, 1), (0, 2, 1), (1, 2, 1), (2, 1, 0)))


ORDER = ((3, 1, 2, 0), (0, 2, 1, 3))


def place(e):
    return e // 2, e % 2, e // 4


def node_place(e):
    x, z, core = place(e)
    return x, z, 1 - core


def comm_kernel(
    pend, panel_in, scale_in, linv_in, out, scaled,
    panel, scale, linv, pown, xin, part, fan, sol, pcol, acc, sums, terms, taken, oblk,
    ready, ld, lp, xs, xr, ps, pr, as_, ar, ls, lr, qs, qr, rs, us, bs, br, ds_, dr, es, er, zs, zr_, ts, fs, fr,
):
    row, col = lax.axis_index("row"), lax.axis_index("col")
    x, z = row // NZ, row % NZ
    y, h = col // 2, col % 2
    other = 2 * y + (1 - h)
    mine = h == x // 2
    lead_chip = z < 2
    lead = jnp.logical_and(lead_chip, mine)
    my_j = jnp.where(z == 0, 0, 1)
    my_e = jnp.where(lead, 2 * x + my_j, -1)
    source = [row == k for k in range(2)]
    my_node = jnp.where(jnp.logical_and(lead_chip, jnp.logical_not(mine)), 2 * x + my_j, -1)
    my_add = jnp.int32(-1)
    add_core = jnp.int32(0)
    for hs in range(2):
        for i, (ax, az, ac) in enumerate(ADDERS[hs]):
            here = jnp.logical_and(row == ax * NZ + az, h == ac)
            my_add = jnp.where(here, i, my_add)
            add_core = jnp.where(here, hs, add_core)

    def add_place(i):
        a, b = ADDERS[0][i], ADDERS[1][i]
        return [jnp.where(h == 0, p, q) for p, q in zip(a, b)]

    adder = my_add >= 0
    before = jnp.logical_or(my_node == 0, my_node == 6)
    behind = jnp.logical_or(my_e == 1, my_e == 7)
    my_node = jnp.where(my_node == 1, -1, my_node)
    my_rows = pl.ds(pl.multiple_of(y * 256, 256), 256)

    def dev(xx, zz, cc):
        return (xx * NZ + zz, cc)

    def solver(e, yy):
        ex, ez, eh = place(e)
        return dev(ex, ez, 2 * yy + eh)

    is_source = jnp.logical_or(source[0], source[1])

    def node(n, yy):
        nx, nz, nh = node_place(n)
        return dev(nx, nz, 2 * yy + nh)

    def lanes(i):
        return pl.ds(pl.multiple_of(i * 128, 128), 128)

    def load(n):
        src, dst = ((panel_in, panel), (scale_in, scale), (linv_in, linv.at[:, pl.ds(0, 128)]))[n]
        return pltpu.make_async_copy(src, dst, ld.at[n])

    def load_own(i):
        return pltpu.make_async_copy(pend.at[:, lanes(4 * h + i)], pown.at[i], lp.at[i])

    load(0).start()
    load(1).start()

    @pl.when(lead)
    def _():
        load(2).start()

    @pl.when(is_source)
    def _():
        for i in range(4):
            load_own(i).start()

    bar = pltpu.get_barrier_semaphore()

    def hello(target):
        pl.semaphore_signal(bar, inc=1, device_id=target, device_id_type=MESH)

    def both(p, q):
        return jnp.logical_and(p, q)

    def no(p):
        return jnp.logical_not(p)

    for yd in range(NY):
        sy = (y + yd) % NY
        if yd:
            @pl.when(lead)
            def _():
                hello((row, 2 * sy + h))
        heads = both(lead, no(behind))

        @pl.when(both(heads, no(source[0])) if yd == 0 else heads)
        def _():
            hello((0, 2 * sy + h))

        @pl.when(before)
        def _():
            hello((0, 2 * sy + 1 - h))

        @pl.when(adder)
        def _():
            hello((1, 2 * sy + add_core))

    for parent, children in CHILDREN.items():
        for child in children:
            @pl.when(my_node == child)
            def _():
                hello(node(parent, y))
    @pl.when(behind)
    def _():
        hello(dev(x, 0, other))

    @pl.when(jnp.logical_or(my_node == 0, my_node == 7))
    def _():
        for hh in range(2):
            hello((1, 2 * y + hh))
    for i in range(4):
        ax, az, ac = add_place(i)
        for yd in range(NY):
            @pl.when(both(both(lead, my_e % 4 == i), y >= yd))
            def _():
                hello(dev(ax, az, 2 * (y - yd) + ac))
    hello((row, other))
    lead_col = 2 * y + x // 2
    line_z = (0, 1)
    away = [(z - lz + NZ) % NZ for lz in line_z]

    def among(v, values):
        hit = v == values[0]
        for w in values[1:]:
            hit = jnp.logical_or(hit, v == w)
        return hit

    direct = [among(a, DIRECT) for a in away]
    relayed = [among(a, RELAYED) for a in away]
    relays = [among(a, (6, 10)) for a in away]
    my_leads = jnp.where(direct[0], 1, 0) + jnp.where(direct[1], 1, 0)
    for j in range(2):
        @pl.when(relayed[j])
        def _():
            step = jnp.where(jnp.logical_or(away[j] == 7, away[j] == 11), NZ - 1, 1)
            hello(dev(x, (z + step) % NZ, col))
        my_leads += jnp.where(relays[j], 2, 0)

    @pl.when(lead)
    def _():
        for d in DIRECT:
            for hh in range(2):
                hello(dev(x, (z + d) % NZ, 2 * y + hh))
    for d in range(1, NX):
        hello(dev((x + d) % NX, z, col))
    expect = 1 + NX - 1 + my_leads + jnp.where(lead, NY - 1, 0)
    expect += jnp.where(source[0], jnp.where(h == 0, 4 * NY - 1, 4 * NY), 0)
    expect += jnp.where(source[1], 4 * NY + 2, 0)
    expect += jnp.where(adder, NY - y, 0) + jnp.where(before, 1, 0)
    for parent, children in CHILDREN.items():
        expect += jnp.where(my_node == parent, len(children), 0)

    def scale_panel():
        load(0).wait()
        load(1).wait()
        for k in range(2):
            active = jnp.where(row > k, 1.0, 0.0)

            def scale_rows(r, c):
                rows = pl.ds(pl.multiple_of(r * 256, 256), 256)
                s = jnp.broadcast_to(scale[k : k + 1, rows] * active, (128, 256)).T
                scaled[rows, k * 128 : (k + 1) * 128] = (panel[rows, k, :].astype(F32) * s).astype(BF)
                return c
            lax.fori_loop(0, 4, scale_rows, 0)

    @pl.when(source[1])
    def _():
        scale_panel()

    pl.semaphore_wait(bar, expect)

    for j in range(2):
        @pl.when(direct[j])
        def _():
            pl.semaphore_signal(
                ready, inc=1, device_id=dev(x, line_z[j], lead_col), device_id_type=MESH)

    def remote(src, dst, send, recv, target):
        return pltpu.make_async_remote_copy(
            src, dst, send, recv, device_id=target, device_id_type=MESH)

    def linv_copy(k):
        return remote(linv_in.at[k], linv.at[k, pl.ds(128, 128)], ls.at[k], lr.at[k], (row, other))

    def swap_copy(i):
        return remote(pend.at[:, lanes(4 * (1 - h) + i)], xin.at[i], xs.at[i], xr.at[i], (row, other))

    def scatter_copy(k, i, yd):
        tx, tz, core = 2 * h + i // 2, (0, h, 0, 1 - h)[i], (h, 1, h, 0)[i]
        if k == 1:
            tx, tz, core = add_place(i)
        ty = (y + yd) % NY
        rows = pl.ds(pl.multiple_of(ty * 256, 256), 256)
        return remote(xin.at[i, rows], part.at[k, yd], ps.at[i, yd], pr.at[k, yd],
                      dev(tx, tz, 2 * ty + core))

    def before_copy():
        return remote(acc, fan.at[0, my_rows], bs, br, dev(x, 1, other))

    def before_wait():
        return remote(acc, fan.at[0, my_rows], bs, br, dev(x, 0, other))

    def panel_block(q):
        return pcol.at[pl.ds((q % 4) * 256, 256), pl.ds((q // 4) * 128, 128)]

    def panel_copy(t, r):
        rows = pl.ds(r * 256, 256)
        target = (node(0, y), (row, other), node(7, y))[t]
        return remote(scaled.at[rows, pl.ds(0, 128)], pcol.at[rows, lanes(h)],
                      qs.at[t, r], qr.at[4 * h + r], target)

    def panel_wait(q):
        return remote(panel_block(q), panel_block(q), qs.at[0, 0], qr.at[q], (row, other))

    def relay_copy(child, n, q):
        return remote(panel_block(q), panel_block(q), rs.at[n, q], qr.at[q], node(child, y))

    def mate_copy(q):
        return remote(panel_block(q), panel_block(q), us.at[q], qr.at[q], (row, other))

    def sums_copy(i, yd):
        tz = i % 2
        return remote(acc, sums.at[my_rows], ds_.at[yd], dr.at[y],
                      dev(2 * add_core + i // 2, tz, 2 * (y + yd) + add_core))

    def sums_wait(sy):
        rows = sums.at[pl.ds(sy * 256, 256)]
        return remote(rows, rows, ds_.at[0], dr.at[sy], (row, other))

    def terms_copy(t):
        rows = pl.ds(0, (t + 1) * 256)
        return remote(terms.at[rows], taken.at[y, rows], es.at[t], er.at[y], (row, 2 * t + h))

    def terms_wait(t, sy):
        rows = taken.at[sy, pl.ds(0, (t + 1) * 256)]
        return remote(rows, rows, es.at[t], er.at[sy], (row, other))

    def gather_copy(buf, n, yd):
        return remote(buf.at[my_rows], buf.at[my_rows], as_.at[n, yd - 1], ar.at[n, yd - 1],
                      (row, 2 * ((y + yd) % NY) + h))

    def piece(k, xx, j):
        return out.at[k, :, lanes(2 * xx + j)]

    def line_copy(k, j, d, same):
        return remote(piece(k, x, j) if same else oblk.at[k], piece(k, x, j),
                      zs.at[k, d, 0 if same else 1], zr_.at[k, j],
                      dev(x, (z + d) % NZ, col if same else other))

    def pass_copy(k, j, n):
        return remote(piece(k, x, j), piece(k, x, j), ts.at[k, n], zr_.at[k, j],
                      dev(x, (z + (1, NZ - 1)[n]) % NZ, col))

    def spread_copy(k, j, d):
        return remote(piece(k, x, j), piece(k, x, j), fs.at[k, j, d - 1], fr.at[k, j, d - 1],
                      dev((x + d) % NX, z, col))

    def spread_wait(k, j, d):
        fx = (x + NX - d) % NX
        return remote(piece(k, fx, j), piece(k, fx, j), fs.at[k, j, d - 1], fr.at[k, j, d - 1],
                      dev(fx, z, col))

    def spread(k):
        for j in range(2):
            @pl.when(no(both(lead, my_j == j)))
            def _():
                line_copy(k, j, 0, False).wait_recv()

            @pl.when(relays[j])
            def _():
                for n in range(2):
                    pass_copy(k, j, n).start()
            for d in (2, 1, 3):
                spread_copy(k, j, d).start()

    def unless_local(k, i, yd, action, local=None):
        if not (k == 0 and i == 0 and yd == 0):
            action()
        else:
            pl.when(h != 0)(action)
            if local:
                pl.when(h == 0)(local)

    @pl.when(both(lead_chip, no(mine)))
    def _():
        for k in range(2):
            linv_copy(k).start()

    @pl.when(is_source)
    def _():
        for k in range(2):
            @pl.when(source[k])
            def _():
                for i in ORDER[k]:
                    swap_copy(i).start()

    @pl.when(source[1])
    def _():
        for r in range(4):
            panel_copy(0, r).start()
            panel_copy(2, r).start()

        @pl.when(h == 0)
        def _():
            pcol[:, 0:128] = scaled[:, 0:128]

        @pl.when(h == 1)
        def _():
            for r in range(4):
                panel_copy(1, r).start()

    for k in range(2):
        @pl.when(source[k])
        def _():
            for i in ORDER[k]:
                load_own(i).wait()
                swap_copy(i).wait_recv()

                def add(r, c):
                    rows = pl.ds(pl.multiple_of(r * 256, 256), 256)
                    xin[i, rows] = (pown[i, rows].astype(F32) + xin[i, rows].astype(F32)).astype(BF)
                    return c
                lax.fori_loop(0, 4, add, 0)

                def keep():
                    part[k, 0] = xin[i, my_rows]
                for yd in (2, 1, 3, 0):
                    unless_local(k, i, yd, lambda: scatter_copy(k, i, yd).start(), keep)

    def reduced(k):
        if k == 1:
            scatter_copy(k, 0, 0).wait_recv()
        else:
            @pl.when(my_e != 0)
            def _():
                scatter_copy(k, 0, 0).wait_recv()
        for yd in range(1, NY):
            scatter_copy(k, 0, yd).wait_recv()
        total = part[k, 0].astype(F32)
        for yd in range(1, NY):
            total += part[k, yd].astype(F32)
        return total

    def gather_start(buf, n):
        for yd in (2, 1, 3):
            gather_copy(buf, n, yd).start()

    def gather_wait(buf, n):
        for yd in range(1, NY):
            gather_copy(buf, n, yd).wait_recv()

    def solve(k, depth):
        blocks = jnp.dot(linv[k, :, :depth], fan[k, :depth], preferred_element_type=F32).astype(BF)
        oblk[k] = blocks[128:]
        out[k, :, lanes(2 * x + my_j)] = blocks[:128]
        return blocks

    def line_start(k):
        for j in range(2):
            @pl.when(my_j == j)
            def _():
                for d in DIRECT:
                    line_copy(k, j, d, False).start()
                    line_copy(k, j, d, True).start()
                line_copy(k, j, 0, False).start()

    def add_up(which):
        @pl.when(both(adder, which))
        def _():
            acc[...] = reduced(1).astype(BF)
            for i in range(4):
                for yd in (2, 1, 3, 0):
                    @pl.when(both(my_add == i, y + yd < NY))
                    def _():
                        sums_copy(i, yd).start()

    @pl.when(before)
    def _():
        acc[...] = reduced(0).astype(BF)
        before_copy().start()

    add_up(my_node != 7)

    @pl.when(my_node >= 0)
    def _():
        for c in (0, 4, 1, 5, 2, 6, 3, 7):
            panel_wait(c).wait_recv()
            for parent, children in CHILDREN.items():
                @pl.when(my_node == parent)
                def _():
                    for n, child in enumerate(children):
                        relay_copy(child, n, c).start()

            mate_copy(c).start()

    @pl.when(lead)
    def _():
        @pl.when(behind)
        def _():
            before_wait().wait_recv()

        @pl.when(no(behind))
        def _():
            fan[0, my_rows] = reduced(0).astype(BF)
        gather_start(fan.at[0], 0)
        for k in range(2):
            linv_copy(k).wait_recv()
        load(2).wait()
        gather_wait(fan.at[0], 0)
        blocks = solve(0, fan.shape[1])
        sol[pl.ds(pl.multiple_of(h * 128, 128), 128)] = blocks[:128]
        sol[pl.ds(pl.multiple_of((1 - h) * 128, 128), 128)] = blocks[128:]
        for q in range(8):
            if q < 4:
                @pl.when(my_e != 1)
                def _():
                    panel_wait(q).wait_recv()
            else:
                panel_wait(q).wait_recv()
        terms[...] = jnp.dot(pcol[...], sol[...], preferred_element_type=F32).astype(BF)
        for t in (3, 2, 1, 0):
            @pl.when(y != t)
            def _():
                terms_copy(t).start()
        pl.semaphore_wait(ready, 2 * len(DIRECT))
        line_start(0)
        spread(0)
        for t in range(NY):
            @pl.when(y == t)
            def _():
                depth = (t + 1) * 256
                for sy in range(t + 1):
                    sums_wait(sy).wait_recv()
                total = sums[:depth].astype(F32) - terms[:depth].astype(F32)
                for sy in range(NY):
                    if sy != t:
                        terms_wait(t, sy).wait_recv()
                        total -= taken[sy, :depth].astype(F32)
                fan[1, :depth] = total.astype(BF)
                solve(1, depth)
        line_start(1)

    @pl.when(no(lead))
    def _():
        add_up(my_node == 7)

        @pl.when(no(source[1]))
        def _():
            scale_panel()
        spread(0)

    @pl.when(both(lead, no(source[1])))
    def _():
        scale_panel()
    spread(1)

    for k in range(2):
        for j in range(2):
            for d in range(1, NX):
                spread_wait(k, j, d).wait_recv()

    for k in range(2):
        for j in range(2):
            for d in range(1, NX):
                spread_copy(k, j, d).wait_send()

            @pl.when(relays[j])
            def _():
                for n in range(2):
                    pass_copy(k, j, n).wait_send()

    @pl.when(both(lead_chip, no(mine)))
    def _():
        for k in range(2):
            linv_copy(k).wait_send()

    for k in range(2):
        @pl.when(source[k])
        def _():
            for i in range(4):
                swap_copy(i).wait_send()
                for yd in range(NY):
                    unless_local(k, i, yd, lambda: scatter_copy(k, i, yd).wait_send())

    @pl.when(source[1])
    def _():
        for r in range(4):
            panel_copy(0, r).wait_send()
            panel_copy(2, r).wait_send()

        @pl.when(h == 1)
        def _():
            for r in range(4):
                panel_copy(1, r).wait_send()

    @pl.when(lead)
    def _():
        for yd in range(1, NY):
            gather_copy(fan.at[0], 0, yd).wait_send()
        for t in range(NY):
            @pl.when(y != t)
            def _():
                terms_copy(t).wait_send()
        for k in range(2):
            for d in DIRECT:
                line_copy(k, 0, d, False).wait_send()
                line_copy(k, 0, d, True).wait_send()
            line_copy(k, 0, 0, False).wait_send()
    @pl.when(before)
    def _():
        before_copy().wait_send()

    @pl.when(adder)
    def _():
        for yd in range(NY):
            @pl.when(y + yd < NY)
            def _():
                sums_copy(0, yd).wait_send()

    @pl.when(my_node >= 0)
    def _():
        for c in range(8):
            for parent, children in CHILDREN.items():
                @pl.when(my_node == parent)
                def _():
                    for n, child in enumerate(children):
                        relay_copy(child, n, c).wait_send()

            mate_copy(c).wait_send()


def update_kernel(pend, scaled, solved, out, solved_out, done, sem):
    tiles = done.shape[0]
    size = done.shape[2]
    last = pltpu.make_async_copy(solved, solved_out, sem.at[tiles])
    last.start()

    def store(i):
        return pltpu.make_async_copy(
            done.at[i], out.at[:, pl.ds(pl.multiple_of(i * size, size), size)], sem.at[i])

    def tile(i, c):
        cols = pl.ds(pl.multiple_of(i * size, size), size)
        term = jnp.dot(scaled[...], solved[:, cols], preferred_element_type=F32)
        done[i] = (pend[:, cols].astype(F32) - term).astype(BF)
        store(i).start()
        return c
    lax.fori_loop(0, tiles, tile, 0)
    for i in range(tiles):
        store(i).wait()
    last.wait()


def body(pending, panel, panel_scale, inverse_blocks):
    rows, _, cols = pending.shape
    current = pending.reshape(rows, cols)
    vmem = pl.BlockSpec(memory_space=pltpu.VMEM)
    hbm = pl.BlockSpec(memory_space=pltpu.HBM)
    dma = pltpu.SemaphoreType.DMA
    solved, scaled = pl.pallas_call(
        comm_kernel,
        out_shape=(jax.ShapeDtypeStruct((2, 128, cols), BF), jax.ShapeDtypeStruct((rows, 256), BF)),
        in_specs=[hbm] * 4,
        out_specs=(vmem, vmem),
        scratch_shapes=[
            pltpu.VMEM((rows, 2, 128), BF),
            pltpu.VMEM((2, rows), F32),
            pltpu.VMEM((2, 256, rows), BF),
            pltpu.VMEM((4, rows, 128), BF),
            pltpu.VMEM((4, rows, 128), BF),
            pltpu.VMEM((2, NY, 256, 128), BF),
            pltpu.VMEM((2, rows, 128), BF),
            pltpu.VMEM((256, 128), BF),
            pltpu.VMEM((rows, 256), BF),
            pltpu.VMEM((256, 128), BF),
            pltpu.VMEM((rows, 128), BF),
            pltpu.VMEM((rows, 128), BF),
            pltpu.VMEM((NY, rows, 128), BF),
            pltpu.VMEM((2, 128, 128), BF),
            pltpu.SemaphoreType.REGULAR, dma((3,)), dma((4,)),
            dma((4,)), dma((4,)), dma((4, NY)), dma((2, NY)),
            dma((1, NY - 1)), dma((1, NY - 1)), dma((2,)), dma((2,)),
            dma((3, 4)), dma((8,)), dma((2, 8)), dma((8,)), dma, dma, dma((NY,)), dma((NY,)),
            dma((NY,)), dma((NY,)),
            dma((2, NZ, 2)), dma((2, 2)), dma((2, 2)), dma((2, 2, NX - 1)), dma((2, 2, NX - 1)),
        ],
        compiler_params=pltpu.CompilerParams(
            collective_id=0, has_side_effects=True, vmem_limit_bytes=32 << 20),
        name="substitute",
    )(*(pltpu.with_memory_space_constraint(v, pltpu.HBM)
        for v in (current, panel, panel_scale.T, inverse_blocks)))
    remaining, solved = pl.pallas_call(
        update_kernel,
        out_shape=(jax.ShapeDtypeStruct((rows, cols), BF), jax.ShapeDtypeStruct((256, cols), BF)),
        in_specs=[vmem] * 3,
        out_specs=(hbm, hbm),
        scratch_shapes=[pltpu.VMEM((4, rows, cols // 4), BF), dma((5,))],
        compiler_params=pltpu.CompilerParams(vmem_limit_bytes=32 << 20),
        name="update",
    )(current, scaled, solved.reshape(256, cols))
    return remaining[:, None, :], solved.reshape(2, 128, cols)


def solution(mesh):
    placed = (P("row", "col", None), P("row", None, "col"), P("row", None), P(None, "col", None))
    return jax.shard_map(
        body,
        mesh=mesh,
        in_specs=placed,
        out_specs=(P("row", "col", None), P(None, "col", None)),
        check_vma=False,
    )
```
